32 devices in a mesh: rep: 2 (over x), shard: 16 (over z, y, core).
Axes of the slice: x: 2, y: 2, z: 4, core: 2. Of those that a mesh axis runs over, the one named last changes fastest.
Arguments:
- tokens: bfloat16 [2, 6144, 1024], P('rep', 'shard'), may hold values from -6 to 6
- cotangent: bfloat16 [2, 6144, 1024], P('rep', 'shard'), may hold values from -6 to 6
- seg_ids: int32 [2, 6144], P('rep'), may hold values from 0 to 7, never falling along the last dimension, each value on 1 to 2000 neighbouring positions
- random_blocks: int32 [2, 16, 96, 3], P('rep', 'shard'), may hold values from 0 to 95
- global_blocks: int32 [2, 2], P('rep'), may hold values from 0 to 95
- ln1_gain: bfloat16 [1024], P('shard'), may hold values from 0.5 to 1.5
- ln1_bias: bfloat16 [1024], P('shard'), may hold values from -1.5 to 1.5
- w_query: bfloat16 [1024, 1024], P('shard'), may hold values from -0.1875 to 0.1875
- b_query: bfloat16 [1024], P('shard'), may hold values from -1.5 to 1.5
- w_key: bfloat16 [1024, 1024], P('shard'), may hold values from -0.1875 to 0.1875
- w_value: bfloat16 [1024, 1024], P('shard'), may hold values from -0.1875 to 0.1875
- b_value: bfloat16 [1024], P('shard'), may hold values from -1.5 to 1.5
- w_out: bfloat16 [1024, 1024], P('shard'), may hold values from -2 to 2
- b_out: bfloat16 [1024], P('shard'), may hold values from -1.5 to 1.5
- ln2_gain: bfloat16 [1024], P('shard'), may hold values from 0.5 to 1.5
- ln2_bias: bfloat16 [1024], P('shard'), may hold values from -1.5 to 1.5
- w_up: bfloat16 [1024, 4096], P('shard'), may hold values from -0.1875 to 0.1875
- b_up: bfloat16 [4096], P('shard'), may hold values from -1.5 to 1.5
- w_down: bfloat16 [4096, 1024], P('shard'), may hold values from -0.125 to 0.125
- b_down: bfloat16 [1024], P('shard'), may hold values from -1.5 to 1.5
Outputs:
- layer_out: bfloat16 [2, 6144, 1024], P('rep', 'shard')
- grad_tokens: bfloat16 [2, 6144, 1024], P('rep', 'shard')
- grad_ln1_gain: float32 [1024], P('shard')
- grad_ln1_bias: float32 [1024], P('shard')
- grad_w_query: float32 [1024, 1024], P('shard')
- grad_b_query: float32 [1024], P('shard')
- grad_w_key: float32 [1024, 1024], P('shard')
- grad_w_value: float32 [1024, 1024], P('shard')
- grad_b_value: float32 [1024], P('shard')
- grad_w_out: float32 [1024, 1024], P('shard')
- grad_b_out: float32 [1024], P('shard')
- grad_ln2_gain: float32 [1024], P('shard')
- grad_ln2_bias: float32 [1024], P('shard')
- grad_w_up: float32 [1024, 4096], P('shard')
- grad_b_up: float32 [4096], P('shard')
- grad_w_down: float32 [4096, 1024], P('shard')
- grad_b_down: float32 [1024], P('shard')
The draws below stay inside these ranges and needn't reach their ends.
All inputs are finite; a program needn't handle non-finite values.
Results may differ from the reference program's by a relative error of at most 0.019.
Values may be sent and summed in bfloat16 or wider, within the bound.
No kernel may reach another device: no remote copies, remote signals or barrier semaphores. Data moves between devices by JAX's collectives and lax.ppermute only.
A program may use at most 192 MiB of HBM per device.

```python
import math
import jax
import jax.numpy as jnp
import numpy as np
from jax import lax

D = 1024
H = 16
DH = 64
FF = 4096
BLK = 64
RND = 3
GLB = 2
SEQ = 6144
SEQS = 2
NB = 96
DOCS = 8
DOC_MOST = 2000


def plant(array, key, least, largest):
    longest = array.shape.index(max(array.shape))
    spots = []
    for shift in (0, 1):
        where = [jax.random.randint(jax.random.fold_in(key, axis), (), 0, length) for axis, length in enumerate(array.shape)]
        where[longest] = (where[longest] + shift) % array.shape[longest]
        spots.append(tuple(where))
    return array.at[spots[0]].set(least).at[spots[1]].set(largest)


def level_of(stream_key, shape, cuts, low, top_value):
    gain = 1.0
    for axis_at, parts in cuts:
        steps = jax.random.uniform(jax.random.fold_in(jax.random.fold_in(stream_key, 6), axis_at), (parts,), jnp.float32, low / len(cuts), top_value / len(cuts))
        gain = gain * jnp.repeat(jnp.exp(steps), shape[axis_at] // parts).reshape((-1,) + (1,) * (len(shape) - 1 - axis_at))
    return gain


def profile(count, total, reach, lean):
    weights = [(1 << 20) // math.isqrt(standing ** lean) + 1 for standing in range(2, count + 1)]
    spare, counts = total - reach - (count - 1), [1] * (count - 1)
    while spare > 0:
        free = [i for i in range(count - 1) if counts[i] < reach]
        mass, budget = sum([weights[i] for i in free]), spare
        for i in free:
            extra = min(reach - counts[i], max(1, budget * weights[i] // mass), spare)
            counts[i] = counts[i] + extra
            spare = spare - extra
    return np.array([reach] + counts)


def ragged_sizes(key, number_of, total, reach, skew):
    if number_of == 2:
        one = jax.random.randint(key, (), max(1, total - reach), min(reach, total - 1) + 1)
        return jnp.stack([one, total - one])
    lengths = jnp.asarray(profile(number_of, total, reach, skew), jnp.int32)
    pairs = (number_of - 1) // 2
    giver, receiver = lengths[1:1 + 2 * pairs:2], lengths[2:2 + 2 * pairs:2]
    room = jnp.minimum(giver - 1, reach - receiver)
    shifted = jax.random.randint(jax.random.fold_in(key, 1), (pairs,), 0, 1 << 20) % (room + 1)
    lengths = lengths.at[1:1 + 2 * pairs:2].set(giver - shifted).at[2:2 + 2 * pairs:2].set(receiver + shifted)
    return lengths[jax.random.permutation(jax.random.fold_in(key, 2), number_of)]


def noise(stream_key, shape, scale, most, shards=(), kind=jnp.bfloat16):
    values = scale * jax.random.normal(stream_key, shape, jnp.float32)
    if shards:
        values = values * level_of(stream_key, shape, shards, -0.22, 0.18)
    return jnp.clip(values, -most, most).astype(kind)


def setup_inputs(seed: int = 0) -> dict:
    splits = jax.random.split(jax.random.key(seed), 21)
    return {
        "tokens": noise(splits[0], (SEQS, SEQ, D), 1.0, 6.0, ((0, 2), (1, 16))),
        "cotangent": noise(splits[1], (SEQS, SEQ, D), 1.0, 6.0, ((0, 2), (1, 16))),
        "seg_ids": jax.vmap(lambda own: jnp.searchsorted(jnp.cumsum(ragged_sizes(own, DOCS, SEQ, DOC_MOST, 1)), jnp.arange(SEQ), side="right"))(jax.random.split(splits[2], SEQS)).reshape((SEQS, SEQ)).astype(jnp.int32),
        "random_blocks": plant(jax.random.randint(splits[3], (SEQS, H, NB, RND), 0, NB), jax.random.fold_in(splits[3], 1), 0, NB - 1).astype(jnp.int32),
        "global_blocks": plant(jax.random.randint(splits[4], (SEQS, GLB), 0, NB), jax.random.fold_in(splits[4], 1), 0, NB - 1).astype(jnp.int32),
        "ln1_gain": jnp.clip(1.0 + 0.1 * jax.random.normal(splits[5], (D,), jnp.float32), 0.5, 1.5).astype(jnp.bfloat16),
        "ln1_bias": noise(splits[6], (D,), 0.3, 1.5, ((0, 16),)),
        "w_query": noise(splits[7], (D, D), D ** -0.5, 0.1875, ((0, 16),)),
        "b_query": noise(splits[8], (D,), 0.3, 1.5, ((0, 16),)),
        "w_key": noise(splits[9], (D, D), D ** -0.5, 0.1875, ((0, 16),)),
        "w_value": noise(splits[10], (D, D), D ** -0.5, 0.1875, ((0, 16),)),
        "b_value": noise(splits[11], (D,), 0.3, 1.5, ((0, 16),)),
        "w_out": noise(splits[12], (D, D), (max(D // 128, 2)) ** -0.5, 2.0, ((0, 16),)),
        "b_out": noise(splits[13], (D,), 0.3, 1.5, ((0, 16),)),
        "ln2_gain": jnp.clip(1.0 + 0.1 * jax.random.normal(splits[14], (D,), jnp.float32), 0.5, 1.5).astype(jnp.bfloat16),
        "ln2_bias": noise(splits[15], (D,), 0.3, 1.5, ((0, 16),)),
        "w_up": noise(splits[16], (D, FF), D ** -0.5, 0.1875, ((0, 16),)),
        "b_up": noise(splits[17], (FF,), 0.3, 1.5, ((0, 16),)),
        "w_down": noise(splits[18], (FF, D), (FF // 2) ** -0.5, 0.125, ((0, 16),)),
        "b_down": noise(splits[19], (D,), 0.3, 1.5, ((0, 16),)),
    }


@jax.custom_vjp
def low(v):
    return lax.optimization_barrier(v.astype(jnp.bfloat16)).astype(jnp.float32)

@jax.custom_vjp
def low_back(v):
    return v

def low_keep(v):
    return (low(v), None)

def low_pass(kept, grad):
    return (grad,)

def back_keep(v):
    return (v, None)

def back_low(kept, grad):
    return (low(grad),)
low.defvjp(low_keep, low_pass)
low_back.defvjp(back_keep, back_low)
EPSILON = 1e-05
HIGHEST = lax.Precision.HIGHEST

def layer_norm(values, norm_gain, norm_shift):
    centre = lax.optimization_barrier(jnp.mean(values, axis=-1, keepdims=True))
    centred = values - centre
    spread = lax.optimization_barrier(jnp.mean(centred * centred, axis=-1, keepdims=True))
    return centred * lax.rsqrt(spread + EPSILON) * norm_gain + norm_shift

def matmul(left, right):
    return jnp.dot(left, right, precision=HIGHEST)

def key_blocks(random_heads, global_ids):
    heads_count, blocks_count = (random_heads.shape[0], random_heads.shape[1])
    position = jnp.arange(blocks_count, dtype=jnp.int32)
    window = jnp.stack([position - 1, position, position + 1], axis=1)
    window = jnp.broadcast_to(window[None], (heads_count, blocks_count, 3))
    global_all = jnp.broadcast_to(global_ids[None, None, :].astype(jnp.int32), (heads_count, blocks_count, global_ids.shape[0]))
    listed = jnp.concatenate([window, random_heads.astype(jnp.int32), global_all], axis=2)
    slot_count = listed.shape[2]
    earlier = jnp.arange(slot_count)[:, None] > jnp.arange(slot_count)[None, :]
    repeated = jnp.any((listed[..., :, None] == listed[..., None, :]) & earlier, axis=-1)
    usable = (listed >= 0) & (listed < blocks_count) & jnp.logical_not(repeated)
    return (jnp.clip(listed, 0, blocks_count - 1).astype(jnp.int32), usable)

def pick_blocks(table, chosen):
    return jax.vmap(lambda head_table, head_chosen: head_table[head_chosen])(table, chosen)

def attend_group(query_group, key_table, value_table, seg_query, seg_table, chosen, usable):
    key_group = pick_blocks(key_table, chosen)
    value_group = pick_blocks(value_table, chosen)
    seg_keys = seg_table[chosen]
    factor = 1.0 / math.sqrt(DH)
    scores = low_back(jnp.einsum('hqid,hqkjd->hqikj', query_group, key_group, precision=HIGHEST) * factor)
    allowed = usable[:, :, None, :, None] & (seg_query[None, :, :, None, None] == seg_keys[:, :, None, :, :])
    masked = jnp.where(allowed, scores, -1e+30)
    layout = masked.shape
    chances = jax.nn.softmax(masked.reshape(layout[:3] + (layout[3] * layout[4],)), axis=-1).reshape(layout)
    chances = low(chances)
    return jnp.einsum('hqikj,hqkjd->hqid', chances, value_group, precision=HIGHEST)

def attention(query, keys, values, seg_row, random_heads, global_ids):
    length = query.shape[0]
    blocks_count = length // BLK
    per_group = math.gcd(blocks_count, 16)
    groups_count = blocks_count // per_group

    def heads_major(table):
        return table.reshape(blocks_count, BLK, H, DH).transpose(2, 0, 1, 3)
    query_table = heads_major(query)
    key_table = heads_major(keys)
    value_table = heads_major(values)
    chosen, usable = key_blocks(random_heads, global_ids)
    seg_table = seg_row.reshape(blocks_count, BLK)

    def grouped(table):
        return jnp.moveaxis(table.reshape((table.shape[0], groups_count, per_group) + table.shape[2:]), 1, 0)

    def one_group(pieces):
        query_group, group_chosen, group_usable, seg_query = pieces
        return attend_group(query_group, key_table, value_table, seg_query, seg_table, group_chosen, group_usable)
    outputs = lax.map(jax.checkpoint(one_group), (grouped(query_table), grouped(chosen), grouped(usable), seg_table.reshape(groups_count, per_group, BLK)))
    outputs = jnp.moveaxis(outputs, 0, 1).reshape(H, blocks_count, BLK, DH)
    return outputs.transpose(1, 2, 0, 3).reshape(length, H * DH)

def forward(inputs, weights, seg_row, random_heads, global_ids):
    gain_one, shift_one, weight_query, bias_query, weight_key, weight_value, bias_value, weight_out, bias_out, gain_two, shift_two, weight_up, bias_up, weight_down, bias_down = weights
    normed_one = low(layer_norm(inputs, gain_one, shift_one))
    query = low(low_back(matmul(normed_one, weight_query) + bias_query))
    keys = low(low_back(matmul(normed_one, weight_key)))
    values = low(low_back(matmul(normed_one, weight_value) + bias_value))
    attended = low(low_back(attention(query, keys, values, seg_row, random_heads, global_ids)))
    middle = inputs + low_back(matmul(attended, weight_out) + bias_out)
    normed_two = low(layer_norm(middle, gain_two, shift_two))
    hidden_pre = low_back(matmul(normed_two, weight_up) + bias_up)
    hidden = low(jax.nn.gelu(hidden_pre, approximate=True))
    return middle + low_back(matmul(hidden, weight_down) + bias_down)

def reference(tokens, cotangent, seg_ids, random_blocks, global_blocks, ln1_gain, ln1_bias, w_query, b_query, w_key, w_value, b_value, w_out, b_out, ln2_gain, ln2_bias, w_up, b_up, w_down, b_down):
    params = tuple((member.astype(jnp.float32) for member in (ln1_gain, ln1_bias, w_query, b_query, w_key, w_value, b_value, w_out, b_out, ln2_gain, ln2_bias, w_up, b_up, w_down, b_down)))

    def per_sequence(totals, pieces):
        inputs, incoming, seg_row, random_heads, global_ids = pieces
        result, pullback = jax.vjp(lambda values, weights: forward(values, weights, seg_row, random_heads, global_ids), inputs.astype(jnp.float32), params)
        grad_inputs, grad_params = pullback(incoming.astype(jnp.float32))
        totals = jax.tree.map(jnp.add, totals, grad_params)
        return (totals, (result.astype(jnp.bfloat16), grad_inputs.astype(jnp.bfloat16)))
    zeros_init = tuple((jnp.zeros(member.shape, jnp.float32) for member in params))
    grads, (outputs, grad_inputs) = lax.scan(per_sequence, zeros_init, (tokens, cotangent, seg_ids, random_blocks, global_blocks))
    return (outputs, grad_inputs, grads[0], grads[1], grads[2], grads[3], grads[4], grads[5], grads[6], grads[7], grads[8], grads[9], grads[10], grads[11], grads[12], grads[13], grads[14])
```

```python
import math

import jax
import jax.numpy as jnp
from jax import lax
from jax.experimental import pallas as pl
from jax.experimental.pallas import tpu as pltpu
from jax.sharding import PartitionSpec as P

BLK = 64
DH = 64
SLOTS = 8
EPSILON = 1e-05
FAR = -1e20
BF = jnp.bfloat16
F32 = jnp.float32
VMEM_LIMIT = 56 * 1024 * 1024


def dot_nn(left, right):
    return lax.dot_general(left, right, (((1,), (0,)), ((), ())), preferred_element_type=F32)


def dot_tn(left, right):
    return lax.dot_general(left, right, (((0,), (0,)), ((), ())), preferred_element_type=F32)


def dot_nt(left, right):
    return lax.dot_general(left, right, (((1,), (1,)), ((), ())), preferred_element_type=F32)


def params(*semantics):
    return pltpu.CompilerParams(
        dimension_semantics=semantics if semantics else None, vmem_limit_bytes=VMEM_LIMIT
    )


def lanes_of(shape):
    return lax.broadcasted_iota(jnp.int32, shape, len(shape) - 1)


def normalize(values):
    centre = jnp.mean(values, axis=-1, keepdims=True)
    centred = values - centre
    spread = jnp.mean(centred * centred, axis=-1, keepdims=True)
    scale = lax.rsqrt(spread + EPSILON)
    return centred * scale, scale


def norm_backward(grad, normal, scale, gain):
    scaled = grad * gain
    mean_one = jnp.mean(scaled, axis=-1, keepdims=True)
    mean_two = jnp.mean(scaled * normal, axis=-1, keepdims=True)
    return scale * (scaled - mean_one - normal * mean_two)


def key_blocks(random_heads, global_ids):
    blocks_count = random_heads.shape[0]
    position = jnp.arange(blocks_count, dtype=jnp.int32)
    window = jnp.stack([position - 1, position, position + 1], axis=1)
    global_all = jnp.broadcast_to(global_ids[None, :], (blocks_count, global_ids.shape[0]))
    listed = jnp.concatenate([window, random_heads, global_all], axis=1)
    slot_count = listed.shape[1]
    earlier = jnp.arange(slot_count)[:, None] > jnp.arange(slot_count)[None, :]
    repeated = jnp.any((listed[..., :, None] == listed[..., None, :]) & earlier, axis=-1)
    usable = (listed >= 0) & (listed < blocks_count) & jnp.logical_not(repeated)
    return jnp.where(usable, listed, blocks_count)


def project_kernel(
    tok_ref, w_ref, bias_ref, norm_ref, qext_ref, kext_ref, n_ref, q_ref, k_ref, v_ref
):
    normal, _ = normalize(tok_ref[...].astype(F32))
    normed = (normal * norm_ref[0:1, :] + norm_ref[1:2, :]).astype(BF)
    n_ref[...] = normed
    out = dot_nn(normed, w_ref[...]) + bias_ref[0:1, :]
    out = out.astype(BF).astype(F32)
    both = out[:, :128]
    lane = lanes_of(both.shape)
    q_ref[...] = jnp.where(lane < DH, both * (1.0 / math.sqrt(DH)), qext_ref[...].astype(F32)).astype(BF)
    k_ref[...] = jnp.where(lane < DH, pltpu.roll(both, DH, 1), kext_ref[...].astype(F32)).astype(BF)
    v_ref[...] = out[:, 128:].astype(BF)


def project(tokens, weight, bias, norm_rows, query_extra, key_extra):
    total, width = tokens.shape
    tile = min(512, total)
    row = lambda n: pl.BlockSpec((tile, n), lambda i: (i, 0))
    whole = lambda a: pl.BlockSpec(a.shape, lambda i: (0,) * a.ndim)
    table = jax.ShapeDtypeStruct((total, 128), BF)
    return pl.pallas_call(
        project_kernel,
        grid=(total // tile,),
        in_specs=[row(width), whole(weight), whole(bias), whole(norm_rows), row(128), row(128)],
        out_specs=[row(width), row(128), row(128), row(128)],
        out_shape=[jax.ShapeDtypeStruct((total, width), BF), table, table, table],
        compiler_params=params("arbitrary"),
        name="project",
    )(tokens, weight, bias, norm_rows, query_extra, key_extra)


def load_tables(pairs, sem):
    copies = [
        pltpu.make_async_copy(src, dst, sem.at[i]) for i, (src, dst) in enumerate(pairs)
    ]
    for copy in copies:
        copy.start()
    for copy in copies:
        copy.wait()


def fill_null(k_ref, v_ref, rows):
    lane = lanes_of((BLK, 128))
    k_ref[rows : rows + BLK, :] = jnp.where(
        (lane >= DH) & (lane < DH + 8), FAR, 0.0
    ).astype(BF)
    v_ref[rows : rows + BLK, :] = jnp.zeros((BLK, 128), BF)


def gather_rows(idx_ref, block, ref):
    pieces = []
    for slot in range(SLOTS):
        start = pl.multiple_of(idx_ref[block * SLOTS + slot] * BLK, BLK)
        pieces.append(ref[pl.ds(start, BLK), :])
    return jnp.concatenate(pieces, axis=0)


def softmax_rows(scores):
    top = jnp.max(scores, axis=1, keepdims=True)
    raised = jnp.exp(scores - top)
    return raised * (1.0 / jnp.sum(raised, axis=1, keepdims=True))


def attend_kernel(idx_ref, q_hbm, k_hbm, v_hbm, o_ref, q_ref, k_ref, v_ref, sem):
    rows = q_hbm.shape[0]
    load_tables(
        [
            (q_hbm, q_ref),
            (k_hbm, k_ref.at[pl.ds(0, rows)]),
            (v_hbm, v_ref.at[pl.ds(0, rows)]),
        ],
        sem,
    )
    fill_null(k_ref, v_ref, rows)
    owners, half, _ = o_ref.shape
    per = half // BLK
    lane = lanes_of((BLK, 128))

    def one(block):
        keys = gather_rows(idx_ref, block, k_ref)
        query = q_ref[pl.ds(pl.multiple_of(block * BLK, BLK), BLK), :]
        chances = softmax_rows(dot_nt(query, keys)).astype(BF)
        return dot_nn(chances, gather_rows(idx_ref, block, v_ref))

    def step(owner, carry):
        for part in range(per):
            first = owner * (2 * per) + part
            low, high = one(first), one(first + per)
            o_ref[owner, part * BLK : (part + 1) * BLK, :] = jnp.where(lane < DH, low, high).astype(BF)
        return carry

    lax.fori_loop(0, owners, step, 0)


def attend(idx, query, keys, values, owners):
    rows = query.shape[0]
    anywhere = pl.BlockSpec(memory_space=pl.ANY)
    return pl.pallas_call(
        attend_kernel,
        in_specs=[pl.BlockSpec(memory_space=pltpu.SMEM), anywhere, anywhere, anywhere],
        out_specs=pl.BlockSpec(memory_space=pltpu.VMEM),
        out_shape=jax.ShapeDtypeStruct((owners, rows // owners // 2, 128), BF),
        scratch_shapes=[
            pltpu.VMEM((rows, 128), BF),
            pltpu.VMEM((rows + BLK, 128), BF),
            pltpu.VMEM((rows + BLK, 128), BF),
            pltpu.SemaphoreType.DMA((3,)),
        ],
        compiler_params=params(),
        name="attend",
    )(idx, query, keys, values)


def attend_back_kernel(
    idx_ref, q_hbm, k_hbm, v_hbm, g_hbm, d_ref, q_ref, k_ref, v_ref, g_ref, dk_ref, dv_ref, sem
):
    rows = q_hbm.shape[0]
    load_tables(
        [
            (q_hbm, q_ref),
            (k_hbm, k_ref.at[pl.ds(0, rows)]),
            (v_hbm, v_ref.at[pl.ds(0, rows)]),
            (g_hbm, g_ref),
        ],
        sem,
    )
    fill_null(k_ref, v_ref, rows)
    dk_ref[...] = jnp.zeros_like(dk_ref)
    dv_ref[...] = jnp.zeros_like(dv_ref)
    owners, half, _ = g_ref.shape
    per = half // BLK
    lane = lanes_of((BLK, 128))

    def one(block, grad):
        keys = gather_rows(idx_ref, block, k_ref)
        values = gather_rows(idx_ref, block, v_ref)
        at = pl.ds(pl.multiple_of(block * BLK, BLK), BLK)
        query = q_ref[at, :]
        chances = softmax_rows(dot_nt(query, keys))
        grad_chances = dot_nt(grad, values)
        inner = jnp.sum(chances * grad_chances, axis=1, keepdims=True)
        grad_scores = (chances * (grad_chances - inner)).astype(BF)
        grad_query = dot_nn(grad_scores, keys) * (1.0 / math.sqrt(DH))
        d_ref[at, 0:128] = jnp.where(lane < DH, grad_query, 0.0).astype(BF)
        key_adds = dot_tn(grad_scores, query)
        value_adds = dot_tn(chances.astype(BF), grad)
        for slot in range(SLOTS):
            start = pl.multiple_of(idx_ref[block * SLOTS + slot] * BLK, BLK)
            cut = slice(slot * BLK, (slot + 1) * BLK)
            dk_ref[pl.ds(start, BLK), :] += key_adds[cut]
            dv_ref[pl.ds(start, BLK), :] += value_adds[cut]

    def step(owner, carry):
        for part in range(per):
            first = owner * (2 * per) + part
            grad = g_ref[owner, part * BLK : (part + 1) * BLK, :]
            zero = jnp.zeros_like(grad)
            one(first, jnp.where(lane < DH, grad, zero))
            one(first + per, jnp.where(lane < DH, zero, grad))
        return carry

    lax.fori_loop(0, owners, step, 0)

    chunk = 512

    def finish(i, carry):
        at = pl.ds(pl.multiple_of(i * chunk, chunk), chunk)
        wide = lanes_of((chunk, 128))
        grad_keys = pltpu.roll(dk_ref[at, :], DH, 1)
        grad_query = d_ref[at, 0:128].astype(F32)
        d_ref[at, 0:128] = jnp.where(wide < DH, grad_query, grad_keys).astype(BF)
        grad_values = dv_ref[at, :]
        grad_values = grad_values + pltpu.roll(grad_values, DH, 1)
        d_ref[at, 128:256] = jnp.where(wide < DH, grad_values, 0.0).astype(BF)
        return carry

    lax.fori_loop(0, rows // chunk, finish, 0)


def attend_back(idx, query, keys, values, grads):
    rows = query.shape[0]
    anywhere = pl.BlockSpec(memory_space=pl.ANY)
    return pl.pallas_call(
        attend_back_kernel,
        in_specs=[pl.BlockSpec(memory_space=pltpu.SMEM)] + [anywhere] * 4,
        out_specs=pl.BlockSpec(memory_space=pltpu.VMEM),
        out_shape=jax.ShapeDtypeStruct((rows, 256), BF),
        scratch_shapes=[
            pltpu.VMEM((rows, 128), BF),
            pltpu.VMEM((rows + BLK, 128), BF),
            pltpu.VMEM((rows + BLK, 128), BF),
            pltpu.VMEM(grads.shape, BF),
            pltpu.VMEM((rows + BLK, 128), F32),
            pltpu.VMEM((rows + BLK, 128), F32),
            pltpu.SemaphoreType.DMA((4,)),
        ],
        compiler_params=params(),
        name="attend_back",
    )(idx, query, keys, values, grads)


def middle_kernel(
    att_ref,
    tok_ref,
    cot_ref,
    down_ref,
    up_ref,
    out_w_ref,
    vec_ref,
    lay_ref,
    gm_ref,
    ga_ref,
    gv_ref,
    grads_hbm,
    a_ref,
    mid_ref,
    n2_ref,
    acc_ref,
    gn_ref,
    gd_buf,
    gu_buf,
    sem,
):
    chunk = pl.program_id(0)
    chunks = pl.num_programs(0)
    slot = lax.rem(chunk, 2)
    owners, half, _ = att_ref.shape
    lane = lanes_of((half, 128))
    width = tok_ref.shape[1]
    up_rows = up_ref.shape[1]
    down_block = down_ref.shape[0]
    down_rows = down_ref.shape[1]

    def copies(at, place):
        return (
            pltpu.make_async_copy(
                gd_buf.at[place],
                grads_hbm.at[pl.ds(at * down_block, down_block), pl.ds(0, down_rows)],
                sem.at[0, place],
            ),
            pltpu.make_async_copy(
                gu_buf.at[place],
                grads_hbm.at[:, pl.ds(down_rows + at * up_rows, up_rows)],
                sem.at[1, place],
            ),
        )

    @pl.when(chunk == 0)
    def _():
        for pair in range(owners // 2):
            one = att_ref[2 * pair].astype(F32)
            two = att_ref[2 * pair + 1].astype(F32)
            cut = slice(pair * 128, (pair + 1) * 128)
            a_ref[0:half, cut] = jnp.where(lane < DH, one, pltpu.roll(two, DH, 1)).astype(BF)
            a_ref[half : 2 * half, cut] = jnp.where(lane < DH, pltpu.roll(one, DH, 1), two).astype(BF)
        mid = (
            tok_ref[...].astype(F32)
            + dot_nn(a_ref[...], out_w_ref[...].reshape(width, width))
            + vec_ref[0:1, :]
        )
        mid_ref[...] = mid
        normal, _ = normalize(mid)
        n2_ref[...] = (normal * vec_ref[1:2, :] + vec_ref[2:3, :]).astype(BF)

    @pl.when(chunk >= 2)
    def _():
        for copy in copies(chunk - 2, slot):
            copy.wait()

    w_up = up_ref[...].reshape(width, -1)
    w_down = down_ref[...].reshape(-1, width)
    cot = cot_ref[...]
    n2 = n2_ref[...]
    pre = dot_nn(n2, w_up) + vec_ref[pl.ds(4 + chunk, 1), :]
    root = math.sqrt(2.0 / math.pi)
    square = pre * pre
    bent = jnp.tanh(root * (pre + 0.044715 * (pre * square)))
    hidden = (0.5 * pre * (1.0 + bent)).astype(BF)
    slope = 0.5 * (1.0 + bent) + 0.5 * pre * (1.0 - bent * bent) * (
        root * (1.0 + (3 * 0.044715) * square)
    )
    grad_pre32 = slope * dot_nt(cot, w_down)
    grad_pre = grad_pre32.astype(BF)
    more = dot_nn(hidden, w_down)
    grad_more = dot_nt(grad_pre, w_up)
    first = chunk == 0
    acc_ref[...] = jnp.where(first, more, acc_ref[...] + more)
    gn_ref[...] = jnp.where(first, grad_more, gn_ref[...] + grad_more)
    gv_ref[pl.ds(4 + chunk, 1), :] = jnp.sum(grad_pre.astype(F32), axis=0, keepdims=True)
    gu_buf[slot] = dot_tn(n2, grad_pre).astype(BF).reshape(gu_buf.shape[1:])
    gd_buf[slot] = dot_tn(hidden, cot).astype(BF).reshape(gd_buf.shape[1:])
    for copy in copies(chunk, slot):
        copy.start()

    @pl.when(chunk == chunks - 1)
    def _():
        mid = mid_ref[...]
        lay_ref[...] = (mid + acc_ref[...] + vec_ref[3:4, :]).astype(BF)
        normal, scale = normalize(mid)
        grad = gn_ref[...]
        cot32 = cot.astype(F32)
        grad_mid = cot32 + norm_backward(grad, normal, scale, vec_ref[1:2, :])
        gm_ref[...] = grad_mid
        branch = grad_mid.astype(BF)
        gv_ref[0:1, :] = jnp.sum(branch.astype(F32), axis=0, keepdims=True)
        gv_ref[1:2, :] = jnp.sum(grad * normal, axis=0, keepdims=True)
        gv_ref[2:3, :] = jnp.sum(grad, axis=0, keepdims=True)
        gv_ref[3:4, :] = jnp.sum(cot32, axis=0, keepdims=True)
        grad_att = dot_nt(branch, out_w_ref[...].reshape(width, width))
        for pair in range(owners // 2):
            cut = slice(pair * 128, (pair + 1) * 128)
            top, low = grad_att[0:half, cut], grad_att[half : 2 * half, cut]
            ga_ref[2 * pair] = jnp.where(lane < DH, top, pltpu.roll(low, DH, 1)).astype(BF)
            ga_ref[2 * pair + 1] = jnp.where(lane < DH, pltpu.roll(top, DH, 1), low).astype(BF)
        for copy in copies(chunk - 1, 1 - slot):
            copy.wait()
        gu_buf[1 - slot] = dot_tn(a_ref[...], branch).astype(BF).reshape(gu_buf.shape[1:])
        last = pltpu.make_async_copy(
            gu_buf.at[1 - slot],
            grads_hbm.at[:, pl.ds(down_rows + chunks * up_rows, up_rows)],
            sem.at[1, 1 - slot],
        )
        last.start()
        for copy in copies(chunk, slot):
            copy.wait()
        last.wait()


def middle(attended, tokens, cotangent, weights, vectors):
    owners, per_owner, width = weights.shape
    count = tokens.shape[0]
    up_rows = width // owners
    chunks = (per_owner - up_rows) // (2 * up_rows)
    down_rows = chunks * up_rows
    down_block = owners // chunks
    whole = lambda a: pl.BlockSpec(a.shape, lambda c: (0,) * a.ndim)
    full = lambda s: pl.BlockSpec(s, lambda c: (0,) * len(s))
    first_up = down_rows // up_rows
    return pl.pallas_call(
        middle_kernel,
        grid=(chunks,),
        in_specs=[
            whole(attended),
            whole(tokens),
            whole(cotangent),
            pl.BlockSpec((down_block, down_rows, width), lambda c: (c, 0, 0)),
            pl.BlockSpec((owners, up_rows, width), lambda c: (0, first_up + c, 0)),
            pl.BlockSpec((owners, up_rows, width), lambda c: (0, first_up + chunks, 0)),
            whole(vectors),
        ],
        out_specs=[
            full((count, width)),
            full((count, width)),
            full(attended.shape),
            full((8, width)),
            pl.BlockSpec(memory_space=pl.ANY),
        ],
        out_shape=[
            jax.ShapeDtypeStruct((count, width), BF),
            jax.ShapeDtypeStruct((count, width), F32),
            jax.ShapeDtypeStruct(attended.shape, BF),
            jax.ShapeDtypeStruct((8, width), F32),
            jax.ShapeDtypeStruct(weights.shape, BF),
        ],
        scratch_shapes=[
            pltpu.VMEM((count, width), BF),
            pltpu.VMEM((count, width), F32),
            pltpu.VMEM((count, width), BF),
            pltpu.VMEM((count, width), F32),
            pltpu.VMEM((count, width), F32),
            pltpu.VMEM((2, down_block, down_rows, width), BF),
            pltpu.VMEM((2, owners, up_rows, width), BF),
            pltpu.SemaphoreType.DMA((2, 2)),
        ],
        compiler_params=params("arbitrary"),
        name="middle",
    )(attended, tokens, cotangent, weights, weights, weights, vectors)


def project_back_kernel(n_ref, d_ref, w_ref, part_ref, dw_ref, db_ref):
    grads = d_ref[...]
    part_ref[...] = dot_nt(grads, w_ref[...]).astype(BF)
    more = dot_tn(n_ref[...], grads)
    sums = jnp.broadcast_to(jnp.sum(grads.astype(F32), axis=0, keepdims=True), db_ref.shape)

    @pl.when(pl.program_id(0) == 0)
    def _():
        dw_ref[...] = more
        db_ref[...] = sums

    @pl.when(pl.program_id(0) > 0)
    def _():
        dw_ref[...] += more
        db_ref[...] += sums


def project_back(normed, grads, weight):
    total, width = normed.shape
    tile = min(512, total)
    row = lambda n: pl.BlockSpec((tile, n), lambda i: (i, 0))
    whole = lambda s: pl.BlockSpec(s, lambda i: (0,) * len(s))
    return pl.pallas_call(
        project_back_kernel,
        grid=(total // tile,),
        in_specs=[row(width), row(256), whole(weight.shape)],
        out_specs=[row(width), whole((width, 256)), whole((8, 256))],
        out_shape=[
            jax.ShapeDtypeStruct((total, width), BF),
            jax.ShapeDtypeStruct((width, 256), F32),
            jax.ShapeDtypeStruct((8, 256), F32),
        ],
        compiler_params=params("arbitrary"),
        name="project_back",
    )(normed, grads, weight)


def last_kernel(tok_ref, gn_ref, gm_ref, norm_ref, out_ref):
    normal, scale = normalize(tok_ref[...].astype(F32))
    grad = norm_backward(gn_ref[...].astype(F32), normal, scale, norm_ref[0:1, :])
    out_ref[...] = (gm_ref[...] + grad).astype(BF)


def last(tokens, grad_normed, grad_middle, norm_rows):
    return pl.pallas_call(
        last_kernel,
        out_shape=jax.ShapeDtypeStruct(tokens.shape, BF),
        compiler_params=params(),
        name="last",
    )(tokens, grad_normed, grad_middle, norm_rows)


def exchange(table):
    return lax.all_to_all(table, "shard", split_axis=0, concat_axis=0, tiled=True)


def over_rep(table):
    reps = lax.axis_size("rep")
    if reps == 1:
        return table.astype(F32)
    if reps == 2:
        other = lax.ppermute(table, "rep", [(0, 1), (1, 0)])
        return table.astype(F32) + other.astype(F32)
    return lax.psum(table, "rep").astype(F32)


def local(
    tokens,
    cotangent,
    seg_ids,
    random_blocks,
    global_blocks,
    ln1_gain,
    ln1_bias,
    w_query,
    b_query,
    w_key,
    w_value,
    b_value,
    w_out,
    b_out,
    ln2_gain,
    ln2_bias,
    w_up,
    b_up,
    w_down,
    b_down,
):
    tokens, cotangent, seg_row = tokens[0], cotangent[0], seg_ids[0]
    count, width = tokens.shape
    owners = lax.axis_size("shard")
    own = width // owners
    hidden = w_up.shape[1]
    chunks = hidden // width

    tiles = jnp.concatenate(
        [w.reshape(own, owners, DH) for w in (w_query, w_key, w_value)], axis=2
    ).transpose(1, 0, 2)
    small = jnp.concatenate([b_out, ln2_gain, ln2_bias, b_down, ln1_gain, ln1_bias, b_up])
    small = jnp.pad(small, (0, own * DH - small.shape[0])).reshape(1, own, DH)
    sent = jnp.concatenate([tiles, jnp.broadcast_to(small, (owners, own, DH))], axis=2)
    got = exchange(sent)
    weight = jnp.concatenate([got[:, :, : 3 * DH], got[:, :, 2 * DH : 3 * DH]], axis=2)
    weight = weight.reshape(width, 4 * DH)
    rows = got[:, :, 3 * DH :].reshape(owners, own * DH)[:, : 6 * own + hidden // owners]
    rows = rows.astype(F32)
    fixed = rows[:, : 6 * own].reshape(owners, 6, own).transpose(1, 0, 2).reshape(6, width)
    up_bias = rows[:, 6 * own :].reshape(chunks, width)
    vectors = jnp.concatenate([fixed[:4], up_bias], axis=0)
    norm_rows = jnp.pad(fixed[4:6], ((0, 6), (0, 0)))
    zero = jnp.zeros((DH,), F32)
    bias = jnp.concatenate([b_query.astype(F32), zero, b_value.astype(F32), b_value.astype(F32)])
    bias = jnp.broadcast_to(bias[None], (8, 4 * DH))

    everyone = lax.all_gather(tokens, "shard", axis=0, tiled=True)
    mine = jnp.concatenate(
        [
            w_down,
            w_up.reshape(own, chunks, width).transpose(1, 0, 2).reshape(own * chunks, width),
            w_out,
        ],
        axis=0,
    )
    weights = lax.all_gather(mine, "shard", axis=0)

    lane = jnp.arange(128, dtype=jnp.int32)[None, :] - DH
    seg_column = seg_row[:, None]
    same = lane == seg_column
    query_extra = same.astype(BF)
    key_extra = jnp.where((lane >= 0) & (lane < 8) & ~same, FAR, 0.0).astype(BF)
    idx = key_blocks(random_blocks[0, 0], global_blocks[0]).reshape(-1)

    normed, query, keys, values = project(
        everyone, weight, bias, norm_rows, query_extra, key_extra
    )
    attended = exchange(attend(idx, query, keys, values, owners))
    layer_out, grad_middle, grad_attended, grad_rows, grads = middle(
        attended, tokens, cotangent, weights, vectors
    )
    shares = lax.psum_scatter(
        grads.reshape(-1, width), "shard", scatter_dimension=0, tiled=True
    )
    grad_table = attend_back(idx, query, keys, values, exchange(grad_attended))
    part, grad_weight, grad_bias = project_back(normed, grad_table, weight)
    grad_normed = lax.psum_scatter(part, "shard", scatter_dimension=0, tiled=True)
    grad_tokens = last(tokens, grad_normed, grad_middle, norm_rows)

    used = weight.astype(F32)[:, : 3 * DH]
    sums = grad_bias[0:1, : 3 * DH]
    spread = grad_weight[:, : 3 * DH] - fixed[5][:, None] * sums
    grad_gain = jnp.sum(used * spread, axis=1) / fixed[4]
    grad_shift = jnp.sum(used * sums, axis=1)
    lines = jnp.concatenate([grad_rows[:4], grad_gain[None], grad_shift[None]], axis=0)
    lines = lines.reshape(6, owners, own).transpose(1, 0, 2).reshape(owners, 6 * own)
    lines = jnp.concatenate([lines, grad_rows[4:].reshape(owners, hidden // owners)], axis=1)
    length = lines.shape[1]
    lines = jnp.pad(lines, ((0, 0), (0, own * DH - length))).reshape(owners, own, DH)
    back = jnp.concatenate(
        [grad_weight[:, : 3 * DH].reshape(owners, own, 3 * DH), lines], axis=2
    ).astype(BF)
    back = exchange(back)
    back_sum = jnp.sum(back[:, :, 3 * DH :].astype(F32), axis=0).reshape(own * DH)[:length]
    heads = over_rep(back[:, :, : 3 * DH])
    heads = heads.transpose(1, 2, 0).reshape(own, 3, DH, owners).transpose(1, 0, 3, 2)
    heads = heads.reshape(3, own, width)
    tail = over_rep(
        jnp.concatenate([back_sum, grad_bias[0, :DH], grad_bias[0, 2 * DH : 3 * DH]]).astype(BF)
    )
    piece = lambda i: tail[i * own : (i + 1) * own]
    shares = over_rep(shares)
    down_rows = chunks * own
    grad_down = shares[:down_rows]
    grad_up = shares[down_rows : 2 * down_rows].reshape(chunks, own, width)
    grad_up = grad_up.transpose(1, 0, 2).reshape(own, hidden)
    grad_out = shares[2 * down_rows :]
    return (
        layer_out[None],
        grad_tokens[None],
        piece(4),
        piece(5),
        heads[0],
        tail[length : length + DH],
        heads[1],
        heads[2],
        tail[length + DH :],
        grad_out,
        piece(0),
        piece(1),
        piece(2),
        grad_up,
        tail[6 * own : length],
        grad_down,
        piece(3),
    )


def solution(mesh):
    rows = P("rep", "shard", None)
    one, two = P("shard"), P("shard", None)
    return jax.shard_map(
        local,
        mesh=mesh,
        in_specs=(
            rows, rows, P("rep", None), P("rep", "shard", None, None), P("rep", None),
            one, one, two, one, two, two, one, two, one, one, one, two, one, two, one,
        ),
        out_specs=(
            rows, rows, one, one, two, one, two, two, one, two, one, one, one, two, one, two, one,
        ),
        check_vma=False,
    )
```

```python
import functools
import math

import jax
import jax.numpy as jnp
from jax import lax
from jax.experimental import pallas as pl
from jax.experimental.pallas import tpu as pltpu
from jax.sharding import PartitionSpec as P

BLK = 64
DH = 64
SLOTS = 8
EPSILON = 1e-05
FAR = -1e20
BF = jnp.bfloat16
F32 = jnp.float32
VMEM_LIMIT = 56 * 1024 * 1024


def dot_nn(left, right):
    return lax.dot_general(left, right, (((1,), (0,)), ((), ())), preferred_element_type=F32)


def dot_tn(left, right):
    return lax.dot_general(left, right, (((0,), (0,)), ((), ())), preferred_element_type=F32)


def dot_nt(left, right):
    return lax.dot_general(left, right, (((1,), (1,)), ((), ())), preferred_element_type=F32)


def params(*semantics):
    return pltpu.CompilerParams(
        dimension_semantics=semantics if semantics else None, vmem_limit_bytes=VMEM_LIMIT
    )


def lanes_of(shape):
    return lax.broadcasted_iota(jnp.int32, shape, len(shape) - 1)


def normalize(values):
    centre = jnp.mean(values, axis=-1, keepdims=True)
    centred = values - centre
    spread = jnp.mean(centred * centred, axis=-1, keepdims=True)
    scale = lax.rsqrt(spread + EPSILON)
    return centred * scale, scale


def norm_backward(grad, normal, scale, gain):
    scaled = grad * gain
    mean_one = jnp.mean(scaled, axis=-1, keepdims=True)
    mean_two = jnp.mean(scaled * normal, axis=-1, keepdims=True)
    return scale * (scaled - mean_one - normal * mean_two)


def key_blocks(random_heads, global_ids):
    blocks_count = random_heads.shape[0]
    position = jnp.arange(blocks_count, dtype=jnp.int32)
    window = jnp.stack([position - 1, position, position + 1], axis=1)
    global_all = jnp.broadcast_to(global_ids[None, :], (blocks_count, global_ids.shape[0]))
    listed = jnp.concatenate([window, random_heads, global_all], axis=1)
    slot_count = listed.shape[1]
    earlier = jnp.arange(slot_count)[:, None] > jnp.arange(slot_count)[None, :]
    repeated = jnp.any((listed[..., :, None] == listed[..., None, :]) & earlier, axis=-1)
    usable = (listed >= 0) & (listed < blocks_count) & jnp.logical_not(repeated)
    return jnp.where(usable, listed, blocks_count)


def ring_of(mesh):
    chips = [devices[0] for devices in mesh.devices.reshape(-1, mesh.shape["shard"])[0].reshape(-1, 2)]
    count = len(chips)
    at = [getattr(chip, "coords", None) for chip in chips]
    if any(c is None for c in at):
        return tuple(range(count))
    near = lambda i, j: sum(abs(p - q) for p, q in zip(at[i], at[j])) == 1

    def grow(path):
        if len(path) == count:
            return path if near(path[-1], path[0]) else None
        for chip in range(count):
            if chip not in path and near(path[-1], chip):
                found = grow(path + [chip])
                if found:
                    return found
        return None

    return tuple(grow([0]) or range(count))


class Ring:
    def __init__(self, order):
        self.order = order
        self.count = len(order)
        self.far = self.count // 2
        self.stages = [[(0, 0), (0, 1)]]
        for k in range(1, self.far):
            self.stages.append([(k, 0), (self.count - k, 0), (k, 1), (self.count - k, 1)])
        self.stages.append([(self.far, 0), (self.far, 1)])
        self.pieces = [piece for stage in self.stages for piece in stage]

    def hop(self, table, by):
        pairs = [
            (2 * self.order[i] + core, 2 * self.order[(i + by) % self.count] + core)
            for i in range(self.count)
            for core in range(2)
        ]
        return lax.ppermute(table, "shard", pairs)

    def swap(self, table):
        return lax.ppermute(table, "shard", [(s, s ^ 1) for s in range(2 * self.count)])

    def sources(self):
        me = lax.axis_index("shard")
        order = jnp.array(self.order, jnp.int32)
        chip, core = me // 2, me % 2
        place = jnp.sum(jnp.where(order == chip, jnp.arange(self.count, dtype=jnp.int32), 0))
        ahead = jnp.array([k for k, _ in self.pieces], jnp.int32)
        other = jnp.array([e for _, e in self.pieces], jnp.int32)
        wanted = (place + ahead) % self.count
        found = jnp.sum(
            jnp.where(wanted[:, None] == jnp.arange(self.count, dtype=jnp.int32)[None], order[None], 0), axis=1
        )
        return 2 * found + jnp.bitwise_xor(core, other)

    def gather(self, table, use, ready):
        tie = lax.optimization_barrier
        half = table.shape[0] // 2
        used = []
        behind = ahead = table
        stages = [[table, self.swap(table)]]
        for k in range(1, self.far + 1):
            if k < self.far:
                ahead, behind = tie((self.hop(ahead, -1), self.hop(behind, 1)))
            else:
                ahead, behind = tie((self.hop(ahead[:half], -1), self.hop(behind[half:], 1)))
            if k == 2:
                ahead, behind, ready = tie((ahead, behind, ready))
            if k >= 2:
                used = used + [use(k - 2, stages[k - 2], ready)]
                ahead, behind, used = tie((ahead, behind, used))
            if k < self.far:
                stages.append([ahead, behind, self.swap(ahead), self.swap(behind)])
        both = jnp.concatenate([ahead, behind], axis=0)
        stages.append([both, self.swap(both)])
        return used + [use(i, stages[i], ready) for i in range(len(used), len(stages))], ahead

    def scatter_order(self):
        n, far = self.count, self.far
        return [far] + [k for near in range(far - 1, 0, -1) for k in (near, n - near)] + [0]

    def scatter_sum(self, own, other, release, finish):
        low = lambda t: t.astype(BF)
        n, far = self.count, self.far
        swapped = {k: self.swap(other[k]) for k in self.scatter_order()}
        own = {k: own[k].astype(F32) + swapped[k].astype(F32) for k in own}
        half = own[far].shape[0] // 2
        start = release(low(own[far]))
        up, down = self.hop(start[:half], 1), self.hop(start[half:], -1)
        blank = jnp.zeros(up.shape, F32)
        up = jnp.concatenate([up.astype(F32), blank], axis=0)
        down = jnp.concatenate([blank, down.astype(F32)], axis=0)
        for k in range(far - 1, 0, -1):
            up, down = low(own[k] + up), low(own[n - k] + down)
            if k == 1:
                up = finish(up)
            up, down = lax.optimization_barrier((up, down))
            up, down = self.hop(up, 1).astype(F32), self.hop(down, -1).astype(F32)
        return own[0] + up + down


def project_kernel(count, *refs):
    tokens, (seg_ref, w_ref, bias_ref, norm_ref), outs = refs[:count], refs[count : count + 4], refs[count + 4 :]
    n_ref, q_ref, k_ref, v_ref = outs
    for i, tok_ref in enumerate(tokens):
        length = tok_ref.shape[0]
        cut = slice(i * length, (i + 1) * length)
        normal, _ = normalize(tok_ref[...].astype(F32))
        normed = (normal * norm_ref[0:1, :] + norm_ref[1:2, :]).astype(BF)
        n_ref[cut] = normed
        out = dot_nn(normed, w_ref[...]) + bias_ref[0:1, :]
        out = out.astype(BF).astype(F32)
        both = out[:, :128]
        lane = lanes_of(both.shape)
        seg = jnp.broadcast_to(seg_ref[i : i + 1, :].astype(F32), (128, length)).T
        same = seg == (lane - DH).astype(F32)
        key_extra = jnp.where((lane < DH + 8) & ~same, FAR, 0.0)
        query = jnp.where(lane < DH, both * (1.0 / math.sqrt(DH)), jnp.where(same, 1.0, 0.0))
        q_ref[cut] = query.astype(BF)
        k_ref[cut] = jnp.where(lane < DH, pltpu.roll(both, DH, 1), key_extra).astype(BF)
        v_ref[cut] = out[:, 128:].astype(BF)


def project(pieces, segs, weight, bias, norm_rows):
    length, width = pieces[0].shape
    total = length * len(pieces)
    table = jax.ShapeDtypeStruct((total, 128), BF)
    return pl.pallas_call(
        functools.partial(project_kernel, len(pieces)),
        out_shape=[jax.ShapeDtypeStruct((total, width), BF), table, table, table],
        compiler_params=params(),
        name="project",
    )(*pieces, segs, weight, bias, norm_rows)


def load_tables(pairs, sem):
    copies = []
    for sources, dst in pairs:
        start = 0
        for src in sources:
            count = src.shape[0]
            place = sem.at[len(copies)]
            copies.append(pltpu.make_async_copy(src, dst.at[pl.ds(start, count)], place))
            start += count
    for copy in copies:
        copy.start()
    for copy in copies:
        copy.wait()


def fill_null(k_ref, v_ref, rows):
    lane = lanes_of((BLK, 128))
    k_ref[rows : rows + BLK, :] = jnp.where(
        (lane >= DH) & (lane < DH + 8), FAR, 0.0
    ).astype(BF)
    v_ref[rows : rows + BLK, :] = jnp.zeros((BLK, 128), BF)


def starts_of(idx_ref, place_ref, block):
    return [
        pl.multiple_of(place_ref[idx_ref[block * SLOTS + slot]] * BLK, BLK) for slot in range(SLOTS)
    ]


def gather_rows(starts, ref):
    return jnp.concatenate([ref[pl.ds(start, BLK), :] for start in starts], axis=0)


def softmax_rows(scores):
    top = jnp.max(scores, axis=1, keepdims=True)
    raised = jnp.exp(scores - top)
    return raised * (1.0 / jnp.sum(raised, axis=1, keepdims=True))


def attend_kernel(parts, idx_ref, src_ref, place_ref, *refs):
    tables, (o_ref, q_ref, k_ref, v_ref, sem) = refs[: 3 * parts], refs[3 * parts :]
    rows = q_ref.shape[0]
    load_tables(
        [(tables[i * parts : (i + 1) * parts], dst) for i, dst in enumerate((q_ref, k_ref, v_ref))],
        sem,
    )
    fill_null(k_ref, v_ref, rows)
    owners, half, _ = o_ref.shape
    per = half // BLK
    lane = lanes_of((BLK, 128))

    def one(piece, owner, part):
        starts = starts_of(idx_ref, place_ref, owner * (2 * per) + part)
        keys = gather_rows(starts, k_ref)
        query = q_ref[pl.ds(pl.multiple_of((piece * (2 * per) + part) * BLK, BLK), BLK), :]
        chances = softmax_rows(dot_nt(query, keys)).astype(BF)
        return dot_nn(chances, gather_rows(starts, v_ref))

    def step(piece, carry):
        owner = src_ref[piece]
        for part in range(per):
            low, high = one(piece, owner, part), one(piece, owner, part + per)
            o_ref[owner, part * BLK : (part + 1) * BLK, :] = jnp.where(lane < DH, low, high).astype(BF)
        return carry

    lax.fori_loop(0, owners, step, 0)


def attend(scalars, tables, owners):
    parts = len(tables[0])
    rows = sum(t.shape[0] for t in tables[0])
    anywhere = pl.BlockSpec(memory_space=pl.ANY)
    flat = [t for table in tables for t in table]
    return pl.pallas_call(
        functools.partial(attend_kernel, parts),
        in_specs=[pl.BlockSpec(memory_space=pltpu.SMEM)] * 3 + [anywhere] * len(flat),
        out_specs=pl.BlockSpec(memory_space=pltpu.VMEM),
        out_shape=jax.ShapeDtypeStruct((owners, rows // owners // 2, 128), BF),
        scratch_shapes=[
            pltpu.VMEM((rows, 128), BF),
            pltpu.VMEM((rows + BLK, 128), BF),
            pltpu.VMEM((rows + BLK, 128), BF),
            pltpu.SemaphoreType.DMA((len(flat),)),
        ],
        compiler_params=params(),
        name="attend",
    )(*scalars, *flat)


def attend_back_kernel(parts, idx_ref, src_ref, place_ref, *refs):
    tables, (d_ref, q_ref, k_ref, v_ref, g_ref, dk_ref, dv_ref, sem) = (
        refs[: 3 * parts + 1],
        refs[3 * parts + 1 :],
    )
    rows = q_ref.shape[0]
    load_tables(
        [(tables[i * parts : (i + 1) * parts], dst) for i, dst in enumerate((q_ref, k_ref, v_ref))]
        + [(tables[3 * parts :], g_ref)],
        sem,
    )
    fill_null(k_ref, v_ref, rows)
    dk_ref[...] = jnp.zeros_like(dk_ref)
    dv_ref[...] = jnp.zeros_like(dv_ref)
    owners, half, _ = g_ref.shape
    per = half // BLK
    lane = lanes_of((BLK, 128))

    def one(piece, owner, part, grad):
        starts = starts_of(idx_ref, place_ref, owner * (2 * per) + part)
        keys = gather_rows(starts, k_ref)
        values = gather_rows(starts, v_ref)
        at = pl.ds(pl.multiple_of((piece * (2 * per) + part) * BLK, BLK), BLK)
        query = q_ref[at, :]
        chances = softmax_rows(dot_nt(query, keys))
        grad_chances = dot_nt(grad, values)
        inner = jnp.sum(chances * grad_chances, axis=1, keepdims=True)
        grad_scores = (chances * (grad_chances - inner)).astype(BF)
        grad_query = dot_nn(grad_scores, keys) * (1.0 / math.sqrt(DH))
        d_ref[at, 0:128] = jnp.where(lane < DH, grad_query, 0.0).astype(BF)
        key_adds = dot_tn(grad_scores, query)
        value_adds = dot_tn(chances.astype(BF), grad)
        for slot, start in enumerate(starts):
            cut = slice(slot * BLK, (slot + 1) * BLK)
            dk_ref[pl.ds(start, BLK), :] += key_adds[cut]
            dv_ref[pl.ds(start, BLK), :] += value_adds[cut]

    def step(piece, carry):
        owner = src_ref[piece]
        for part in range(per):
            grad = g_ref[owner, part * BLK : (part + 1) * BLK, :]
            zero = jnp.zeros_like(grad)
            one(piece, owner, part, jnp.where(lane < DH, grad, zero))
            one(piece, owner, part + per, jnp.where(lane < DH, zero, grad))
        return carry

    lax.fori_loop(0, owners, step, 0)

    chunk = 512

    def finish(i, carry):
        at = pl.ds(pl.multiple_of(i * chunk, chunk), chunk)
        wide = lanes_of((chunk, 128))
        grad_keys = pltpu.roll(dk_ref[at, :], DH, 1)
        grad_query = d_ref[at, 0:128].astype(F32)
        d_ref[at, 0:128] = jnp.where(wide < DH, grad_query, grad_keys).astype(BF)
        grad_values = dv_ref[at, :]
        grad_values = grad_values + pltpu.roll(grad_values, DH, 1)
        d_ref[at, 128:256] = jnp.where(wide < DH, grad_values, 0.0).astype(BF)
        return carry

    lax.fori_loop(0, rows // chunk, finish, 0)


def attend_back(scalars, tables, grads):
    parts = len(tables[0])
    rows = sum(t.shape[0] for t in tables[0])
    anywhere = pl.BlockSpec(memory_space=pl.ANY)
    flat = [t for table in tables for t in table] + [grads]
    return pl.pallas_call(
        functools.partial(attend_back_kernel, parts),
        in_specs=[pl.BlockSpec(memory_space=pltpu.SMEM)] * 3 + [anywhere] * len(flat),
        out_specs=pl.BlockSpec(memory_space=pltpu.VMEM),
        out_shape=jax.ShapeDtypeStruct((rows, 256), BF),
        scratch_shapes=[
            pltpu.VMEM((rows, 128), BF),
            pltpu.VMEM((rows + BLK, 128), BF),
            pltpu.VMEM((rows + BLK, 128), BF),
            pltpu.VMEM(grads.shape, BF),
            pltpu.VMEM((rows + BLK, 128), F32),
            pltpu.VMEM((rows + BLK, 128), F32),
            pltpu.SemaphoreType.DMA((len(flat),)),
        ],
        compiler_params=params(),
        name="attend_back",
    )(*scalars, *flat)


def pack_heads(table_ref, flat):
    half = flat.shape[0] // 2
    lane = lanes_of((half, 128))
    for pair in range(table_ref.shape[0] // 2):
        cut = slice(pair * 128, (pair + 1) * 128)
        top, low = flat[:half, cut], flat[half:, cut]
        table_ref[2 * pair] = jnp.where(lane < DH, top, pltpu.roll(low, DH, 1)).astype(BF)
        table_ref[2 * pair + 1] = jnp.where(lane < DH, pltpu.roll(top, DH, 1), low).astype(BF)


def unpack_heads(flat_ref, table_ref):
    owners, half, _ = table_ref.shape
    lane = lanes_of((half, 128))
    for pair in range(owners // 2):
        one = table_ref[2 * pair].astype(F32)
        two = table_ref[2 * pair + 1].astype(F32)
        cut = slice(pair * 128, (pair + 1) * 128)
        flat_ref[0:half, cut] = jnp.where(lane < DH, one, pltpu.roll(two, DH, 1)).astype(BF)
        flat_ref[half : 2 * half, cut] = jnp.where(lane < DH, pltpu.roll(one, DH, 1), two).astype(BF)


def out_kernel(att_ref, tok_ref, w_ref, vec_ref, a_ref, mid_ref, n2_ref):
    width = tok_ref.shape[1]
    unpack_heads(a_ref, att_ref)
    mid = (
        tok_ref[...].astype(F32)
        + dot_nn(a_ref[...], w_ref[...].reshape(width, width))
        + vec_ref[0:1, :]
    )
    mid_ref[...] = mid
    normal, _ = normalize(mid)
    n2_ref[...] = (normal * vec_ref[1:2, :] + vec_ref[2:3, :]).astype(BF)


def whole(shape):
    return pl.BlockSpec(shape, lambda c: (0,) * len(shape))


def out_rows(weights):
    owners, rows, width = weights.shape
    own = width // owners
    return pl.BlockSpec((owners, own, width), lambda c: (0, rows // own - 1, 0))


def project_out(attended, tokens, weights, vectors):
    shape = tokens.shape
    return pl.pallas_call(
        out_kernel,
        grid=(1,),
        in_specs=[whole(attended.shape), whole(shape), out_rows(weights), whole(vectors.shape)],
        out_specs=[whole(shape)] * 3,
        out_shape=[
            jax.ShapeDtypeStruct(shape, BF),
            jax.ShapeDtypeStruct(shape, F32),
            jax.ShapeDtypeStruct(shape, BF),
        ],
        compiler_params=params("arbitrary"),
        name="project_out",
    )(attended, tokens, weights, vectors)


def feed_kernel(n2_ref, cot_ref, down_ref, up_ref, vec_ref, out_ref, gn_ref, hid_ref, pre_ref, gb_ref, acc_ref, acc_gn):
    chunk = pl.program_id(0)
    width = n2_ref.shape[1]
    w_up = up_ref[...].reshape(width, -1)
    w_down = down_ref[...].reshape(-1, width)
    pre = dot_nn(n2_ref[...], w_up) + vec_ref[pl.ds(4 + chunk, 1), :]
    root = math.sqrt(2.0 / math.pi)
    square = pre * pre
    bent = jnp.tanh(root * (pre + 0.044715 * (pre * square)))
    hidden = (0.5 * pre * (1.0 + bent)).astype(BF)
    slope = 0.5 * (1.0 + bent) + 0.5 * pre * (1.0 - bent * bent) * (
        root * (1.0 + (3 * 0.044715) * square)
    )
    grad_pre = (slope * dot_nt(cot_ref[...], w_down)).astype(BF)
    hid_ref[...] = hidden
    pre_ref[...] = grad_pre
    gb_ref[pl.ds(chunk, 1), :] = jnp.sum(grad_pre.astype(F32), axis=0, keepdims=True)
    more = dot_nn(hidden, w_down)
    grad_more = dot_nt(grad_pre, w_up)

    @pl.when(chunk == 0)
    def _():
        acc_ref[...] = more
        acc_gn[...] = grad_more

    @pl.when(chunk > 0)
    def _():
        out_ref[...] = (acc_ref[...] + more).astype(out_ref.dtype)
        gn_ref[...] = (acc_gn[...] + grad_more).astype(gn_ref.dtype)


def layout_of(weights):
    owners, rows, width = weights.shape
    own = width // owners
    units = (rows - own) // 2
    chunks = units // own
    return owners, own, width, units, chunks


def feed(normed, cotangent, weights, vectors, kind):
    owners, own, width, units, chunks = layout_of(weights)
    assert chunks == 2
    count = normed.shape[0]
    first_up = units // own
    column = pl.BlockSpec((count, width), lambda c: (0, c))
    wide = jax.ShapeDtypeStruct((count, chunks * width), BF)
    return pl.pallas_call(
        feed_kernel,
        grid=(chunks,),
        in_specs=[
            whole(normed.shape),
            whole(cotangent.shape),
            pl.BlockSpec((owners // chunks, units, width), lambda c: (c, 0, 0)),
            pl.BlockSpec((owners, own, width), lambda c: (0, first_up + c, 0)),
            whole(vectors.shape),
        ],
        out_specs=[whole((count, width))] * 2 + [column, column, whole((8, width))],
        out_shape=[
            jax.ShapeDtypeStruct((count, width), kind),
            jax.ShapeDtypeStruct((count, width), kind),
            wide,
            wide,
            jax.ShapeDtypeStruct((8, width), F32),
        ],
        scratch_shapes=[pltpu.VMEM((count, width), F32), pltpu.VMEM((count, width), F32)],
        compiler_params=params("arbitrary"),
        name="feed",
    )(normed, cotangent, weights, weights, vectors)


def feed_grads_kernel(na_ref, nb_ref, ca_ref, cb_ref, ha_ref, hb_ref, pa_ref, pb_ref, grads_hbm, gd_buf, gu_buf, sem):
    chunk = pl.program_id(0)
    down_block, down_rows = gd_buf.shape[1:3]
    up_rows = gu_buf.shape[2]
    down = dot_tn(ha_ref[...], ca_ref[...]) + dot_tn(hb_ref[...], cb_ref[...])
    gd_buf[chunk] = down.astype(BF).reshape(gd_buf.shape[1:])
    copy_down = lambda c: pltpu.make_async_copy(
        gd_buf.at[c],
        grads_hbm.at[pl.ds(c * down_block, down_block), pl.ds(0, down_rows)],
        sem.at[0, c],
    )
    copy_up = lambda c: pltpu.make_async_copy(
        gu_buf.at[c],
        grads_hbm.at[:, pl.ds(down_rows + c * up_rows, up_rows)],
        sem.at[1, c],
    )
    copy_down(chunk).start()
    up = dot_tn(na_ref[...], pa_ref[...]) + dot_tn(nb_ref[...], pb_ref[...])
    gu_buf[chunk] = up.astype(BF).reshape(gu_buf.shape[1:])
    copy_up(chunk).start()

    @pl.when(chunk == 1)
    def _():
        for c in range(2):
            copy_down(c).wait()
            copy_up(c).wait()


def feed_grads(own_part, other_part, weights):
    owners, own, width, units, chunks = layout_of(weights)
    count = own_part[0].shape[0]
    column = pl.BlockSpec((count, width), lambda c: (0, c))
    inputs = [t for both in zip(own_part, other_part) for t in both]
    return pl.pallas_call(
        feed_grads_kernel,
        grid=(chunks,),
        in_specs=[whole((count, width))] * 4 + [column] * 4,
        out_specs=pl.BlockSpec(memory_space=pl.ANY),
        out_shape=jax.ShapeDtypeStruct(weights.shape, BF),
        scratch_shapes=[
            pltpu.VMEM((chunks, owners // chunks, units, width), BF),
            pltpu.VMEM((chunks, owners, own, width), BF),
            pltpu.SemaphoreType.DMA((2, chunks)),
        ],
        compiler_params=params("arbitrary"),
        name="feed_grads",
    )(*inputs)


def out_back_kernel(
    mid_ref, gn_ref, other_ref, cot_ref, a_ref, w_ref, vec_ref, _, gm_ref, ga_ref, gv_ref, grads_hbm, buf, sem
):
    width = mid_ref.shape[1]
    rows = grads_hbm.shape[1]
    normal, scale = normalize(mid_ref[...])
    grad = gn_ref[...] + other_ref[...].astype(F32)
    cot = cot_ref[...].astype(F32)
    grad_mid = cot + norm_backward(grad, normal, scale, vec_ref[1:2, :])
    gm_ref[...] = grad_mid
    branch = grad_mid.astype(BF)
    pack_heads(ga_ref, dot_nt(branch, w_ref[...].reshape(width, width)))
    buf[...] = dot_tn(a_ref[...], branch).astype(BF).reshape(buf.shape)
    copy = pltpu.make_async_copy(buf, grads_hbm.at[:, pl.ds(rows - buf.shape[1], buf.shape[1])], sem)
    copy.start()
    gv_ref[...] = jnp.zeros_like(gv_ref)
    gv_ref[0:1, :] = jnp.sum(branch.astype(F32), axis=0, keepdims=True)
    gv_ref[1:2, :] = jnp.sum(grad * normal, axis=0, keepdims=True)
    gv_ref[2:3, :] = jnp.sum(grad, axis=0, keepdims=True)
    gv_ref[3:4, :] = jnp.sum(cot, axis=0, keepdims=True)
    copy.wait()


def project_out_back(mid, grad, other, cotangent, flat, weights, vectors, grads):
    owners, own, width, units, chunks = layout_of(weights)
    shape = mid.shape
    packed = (owners, shape[0] // 2, 128)
    anywhere = pl.BlockSpec(memory_space=pl.ANY)
    return pl.pallas_call(
        out_back_kernel,
        grid=(1,),
        in_specs=[whole(shape)] * 5 + [out_rows(weights), whole(vectors.shape), anywhere],
        out_specs=[whole(shape), whole(packed), whole((8, width)), anywhere],
        out_shape=[
            jax.ShapeDtypeStruct(shape, F32),
            jax.ShapeDtypeStruct(packed, BF),
            jax.ShapeDtypeStruct((8, width), F32),
            jax.ShapeDtypeStruct(grads.shape, BF),
        ],
        scratch_shapes=[pltpu.VMEM((owners, own, width), BF), pltpu.SemaphoreType.DMA],
        input_output_aliases={7: 3},
        compiler_params=params("arbitrary"),
        name="project_out_back",
    )(mid, grad, other, cotangent, flat, weights, vectors, grads)


def shares_kernel(starts, d_ref, w_ref, *outs):
    weight = w_ref[...]
    for start, out_ref in zip(starts, outs):
        out_ref[...] = dot_nt(d_ref[start : start + out_ref.shape[0], :], weight).astype(BF)


def head_shares(grad_table, weight, starts, count):
    width = weight.shape[0]
    return pl.pallas_call(
        functools.partial(shares_kernel, starts),
        out_shape=[jax.ShapeDtypeStruct((count, width), BF)] * len(starts),
        compiler_params=params(),
        name="head_shares",
    )(grad_table, weight)


def last_kernel(tok_ref, gn_ref, gm_ref, norm_ref, out_ref):
    normal, scale = normalize(tok_ref[...].astype(F32))
    grad = norm_backward(gn_ref[...], normal, scale, norm_ref[0:1, :])
    out_ref[...] = (gm_ref[...] + grad).astype(BF)


def last(tokens, grad_normed, grad_middle, norm_rows):
    return pl.pallas_call(
        last_kernel,
        out_shape=jax.ShapeDtypeStruct(tokens.shape, BF),
        compiler_params=params(),
        name="last",
    )(tokens, grad_normed, grad_middle, norm_rows)


def exchange(table):
    return lax.all_to_all(table, "shard", split_axis=0, concat_axis=0, tiled=True)


def trade(table):
    reps = lax.axis_size("rep")
    return lax.ppermute(table, "rep", [(r, r ^ 1) for r in range(reps)])


def over_alike(table):
    reps = lax.axis_size("rep")
    if reps == 2:
        return table
    groups = [list(range(first, reps, 2)) for first in range(2)]
    return lax.psum(table, "rep", axis_index_groups=groups)


def local(
    ring,
    tokens,
    cotangent,
    seg_ids,
    random_blocks,
    global_blocks,
    ln1_gain,
    ln1_bias,
    w_query,
    b_query,
    w_key,
    w_value,
    b_value,
    w_out,
    b_out,
    ln2_gain,
    ln2_bias,
    w_up,
    b_up,
    w_down,
    b_down,
):
    tokens, cotangent, seg_row = tokens[0], cotangent[0], seg_ids[0]
    count, width = tokens.shape
    owners = lax.axis_size("shard")
    own = width // owners
    hidden = w_up.shape[1]
    units = hidden // owners // 2
    half = lax.axis_index("rep") % 2

    tiles = jnp.concatenate(
        [w.reshape(own, owners, DH) for w in (w_query, w_key, w_value)], axis=2
    ).transpose(1, 0, 2)
    small = jnp.concatenate([b_out, ln2_gain, ln2_bias, b_down, ln1_gain, ln1_bias, b_up])
    small = jnp.pad(small, (0, own * DH - small.shape[0])).reshape(1, own, DH)
    sent = jnp.concatenate([tiles, jnp.broadcast_to(small, (owners, own, DH))], axis=2)
    got = exchange(sent)
    weight = jnp.concatenate([got[:, :, : 3 * DH], got[:, :, 2 * DH : 3 * DH]], axis=2)
    weight = weight.reshape(width, 4 * DH)
    rows = got[:, :, 3 * DH :].reshape(owners, own * DH)[:, : 6 * own + hidden // owners]
    rows = rows.astype(F32)
    fixed = rows[:, : 6 * own].reshape(owners, 6, own).transpose(1, 0, 2).reshape(6, width)
    up_bias = lax.dynamic_slice_in_dim(rows[:, 6 * own :], half * units, units, axis=1)
    vectors = jnp.concatenate([fixed[:4], up_bias.reshape(2, width), jnp.zeros((2, width), F32)], axis=0)
    norm_rows = jnp.pad(fixed[4:6], ((0, 6), (0, 0)))
    zero = jnp.zeros((DH,), F32)
    bias = jnp.concatenate([b_query.astype(F32), zero, b_value.astype(F32), b_value.astype(F32)])
    bias = jnp.broadcast_to(bias[None], (8, 4 * DH))

    up_half = lax.dynamic_index_in_dim(w_up.reshape(own, owners, 2, units), half, 2, keepdims=False)
    mine = jnp.concatenate(
        [
            lax.dynamic_slice_in_dim(w_down, half * units, units, axis=0),
            up_half.reshape(own, 2, width).transpose(1, 0, 2).reshape(2 * own, width),
            w_out,
        ],
        axis=0,
    )
    other_cotangent = trade(cotangent)

    per = count // BLK
    sources = ring.sources()
    idx = key_blocks(random_blocks[0, 0], global_blocks[0])
    position = jnp.arange(owners, dtype=jnp.int32)
    piece_of = jnp.sum(jnp.where(sources[None] == position[:, None], position[None], 0), axis=1)
    place = piece_of[:, None] * per + jnp.arange(per, dtype=jnp.int32)[None]
    place = jnp.concatenate([place.reshape(-1), jnp.full((1,), owners * per, jnp.int32)])
    scalars = (idx.reshape(-1), sources, place)
    segs = seg_row.reshape(owners, count)[sources]

    def use(stage, pieces, ready):
        first = sum(len(earlier) for earlier in ring.stages[:stage])
        segs_here = jnp.pad(segs[first : first + len(pieces)], ((0, 8 - len(pieces)), (0, 0)))
        return project(pieces, segs_here, *ready)

    projected, late = ring.gather(tokens, use, (weight, bias, norm_rows))
    mine, _ = lax.optimization_barrier((mine, late))
    weights = lax.all_gather(mine, "shard", axis=0)
    projected, other_cotangent = lax.optimization_barrier((projected, other_cotangent))
    tables = [[stage[i] for stage in projected] for i in (1, 2, 3)]
    attended = exchange(attend(scalars, tables, owners))
    flat, mid, normed_two = project_out(attended, tokens, weights, vectors)
    other_normed = trade(normed_two)
    more, grad_two, hid, grad_pre, bias_one = feed(normed_two, cotangent, weights, vectors, F32)
    other_normed, grad_two = lax.optimization_barrier((other_normed, grad_two))
    other_more, other_grad, other_hid, other_pre, bias_two = feed(
        other_normed, other_cotangent, weights, vectors, BF
    )
    other_grad = trade(other_grad)
    other_more = trade(other_more)
    grads = feed_grads(
        (normed_two, cotangent, hid, grad_pre),
        (other_normed, other_cotangent, other_hid, other_pre),
        weights,
    )
    grad_middle, grad_attended, grad_rows, grads = project_out_back(
        mid, grad_two, other_grad, cotangent, flat, weights, vectors, grads
    )
    layer_out = (mid + more + other_more.astype(F32) + fixed[3][None]).astype(BF)
    shares = lax.psum_scatter(
        grads.reshape(-1, width), "shard", scatter_dimension=0, tiled=True
    )
    grad_table = attend_back(scalars, tables, exchange(grad_attended))
    at = {piece: i * count for i, piece in enumerate(ring.pieces)}
    order = ring.scatter_order()
    other_shares = head_shares(grad_table, weight, [at[k, 1] for k in order], count)
    table_later, _ = lax.optimization_barrier((grad_table, other_shares))
    own_shares = head_shares(table_later, weight, [at[k, 0] for k in order], count)
    results = []

    def release(first):
        first, table = lax.optimization_barrier((first, grad_table))
        results.append(weight_grads(table))
        return first

    def weight_grads(table):
        grad_weight, done = 0.0, 0
        for stage in projected:
            normed = stage[0]
            grad_weight = grad_weight + dot_tn(normed, table[done : done + normed.shape[0]])
            done += normed.shape[0]
        return finish_weights(grad_weight, jnp.sum(table.astype(F32), axis=0, keepdims=True))

    def finish(rows):
        tied = lax.optimization_barrier((rows, results[0]))
        results[0] = tied[1]
        return tied[0]

    def finish_weights(grad_weight, grad_bias):
        used = weight.astype(F32)[:, : 3 * DH]
        sums = grad_bias[0:1, : 3 * DH]
        spread = grad_weight[:, : 3 * DH] - fixed[5][:, None] * sums
        grad_gain = jnp.sum(used * spread, axis=1) / fixed[4]
        grad_shift = jnp.sum(used * sums, axis=1)
        lines = jnp.concatenate([grad_rows[:4], grad_gain[None], grad_shift[None]], axis=0)
        lines = lines.reshape(6, owners, own).transpose(1, 0, 2).reshape(owners, 6 * own)
        up_lines = (bias_one[:2] + bias_two[:2]).reshape(owners, units)
        lines = jnp.concatenate([lines, up_lines], axis=1)
        length = lines.shape[1]
        lines = jnp.pad(lines, ((0, 0), (0, own * DH - length))).reshape(owners, own, DH)
        back = jnp.concatenate(
            [grad_weight[:, : 3 * DH].reshape(owners, own, 3 * DH), lines], axis=2
        ).astype(BF)
        back = exchange(back)
        back_sum = jnp.sum(back[:, :, 3 * DH :].astype(F32), axis=0).reshape(own * DH)[:length]
        heads = over_alike(back[:, :, : 3 * DH])
        heads = heads.astype(F32) + trade(heads).astype(F32)
        heads = heads.transpose(1, 2, 0).reshape(own, 3, DH, owners).transpose(1, 0, 3, 2)
        heads = heads.reshape(3, own, width)
        tail = jnp.concatenate([back_sum, grad_bias[0, :DH], grad_bias[0, 2 * DH : 3 * DH]])
        tail = over_alike(tail.astype(BF))
        tail_other = trade(tail).astype(F32)
        tail = tail.astype(F32)
        total = tail + tail_other
        piece = lambda i: total[i * own : (i + 1) * own]

        def in_order(here, there, axis):
            both = [jnp.where(half == 0, here, there), jnp.where(half == 0, there, here)]
            return jnp.stack(both, axis=axis)

        grad_up_bias = in_order(tail[6 * own : length], tail_other[6 * own : length], 0).reshape(-1)
        ours = over_alike(shares)
        theirs = trade(ours)
        ours, theirs = ours.astype(F32), theirs.astype(F32)
        grad_down = in_order(ours[:units], theirs[:units], 0).reshape(2 * units, width)
        up_of = lambda t: t[units : 2 * units].reshape(2, own, width).transpose(1, 0, 2).reshape(
            own, owners, units
        )
        grad_up = in_order(up_of(ours), up_of(theirs), 2).reshape(own, hidden)
        grad_out = ours[2 * units :] + theirs[2 * units :]
        return (
            piece(4),
            piece(5),
            heads[0],
            total[length : length + DH],
            heads[1],
            heads[2],
            total[length + DH :],
            grad_out,
            piece(0),
            piece(1),
            piece(2),
            grad_up,
            grad_up_bias,
            grad_down,
            piece(3),
        )

    grad_normed = ring.scatter_sum(
        dict(zip(order, own_shares)), dict(zip(order, other_shares)), release, finish
    )
    grad_tokens = last(tokens, grad_normed, grad_middle, norm_rows)
    return (layer_out[None], grad_tokens[None], *results[0])


def solution(mesh):
    rows = P("rep", "shard", None)
    one, two = P("shard"), P("shard", None)
    return jax.shard_map(
        functools.partial(local, Ring(ring_of(mesh))),
        mesh=mesh,
        in_specs=(
            rows, rows, P("rep", None), P("rep", "shard", None, None), P("rep", None),
            one, one, two, one, two, two, one, two, one, one, one, two, one, two, one,
        ),
        out_specs=(
            rows, rows, one, one, two, one, two, two, one, two, one, one, one, two, one, two, one,
        ),
        check_vma=False,
    )
```

```python
import functools
import math

import jax
import jax.numpy as jnp
from jax import lax
from jax.experimental import pallas as pl
from jax.experimental.pallas import tpu as pltpu
from jax.sharding import PartitionSpec as P

BLK = 64
DH = 64
SLOTS = 8
EPSILON = 1e-05
FAR = -1e20
BF = jnp.bfloat16
F32 = jnp.float32
VMEM_LIMIT = 56 * 1024 * 1024


def dot_nn(left, right):
    return lax.dot_general(left, right, (((1,), (0,)), ((), ())), preferred_element_type=F32)


def dot_tn(left, right):
    return lax.dot_general(left, right, (((0,), (0,)), ((), ())), preferred_element_type=F32)


def dot_nt(left, right):
    return lax.dot_general(left, right, (((1,), (1,)), ((), ())), preferred_element_type=F32)


def params(*semantics):
    return pltpu.CompilerParams(
        dimension_semantics=semantics if semantics else None, vmem_limit_bytes=VMEM_LIMIT
    )


def lanes_of(shape):
    return lax.broadcasted_iota(jnp.int32, shape, len(shape) - 1)


def normalize(values):
    centre = jnp.mean(values, axis=-1, keepdims=True)
    centred = values - centre
    spread = jnp.mean(centred * centred, axis=-1, keepdims=True)
    scale = lax.rsqrt(spread + EPSILON)
    return centred * scale, scale


def norm_backward(grad, normal, scale, gain):
    scaled = grad * gain
    mean_one = jnp.mean(scaled, axis=-1, keepdims=True)
    mean_two = jnp.mean(scaled * normal, axis=-1, keepdims=True)
    return scale * (scaled - mean_one - normal * mean_two)


def key_blocks(random_heads, global_ids):
    blocks_count = random_heads.shape[0]
    position = jnp.arange(blocks_count, dtype=jnp.int32)
    window = jnp.stack([position - 1, position, position + 1], axis=1)
    global_all = jnp.broadcast_to(global_ids[None, :], (blocks_count, global_ids.shape[0]))
    listed = jnp.concatenate([window, random_heads, global_all], axis=1)
    slot_count = listed.shape[1]
    earlier = jnp.arange(slot_count)[:, None] > jnp.arange(slot_count)[None, :]
    repeated = jnp.any((listed[..., :, None] == listed[..., None, :]) & earlier, axis=-1)
    usable = (listed >= 0) & (listed < blocks_count) & jnp.logical_not(repeated)
    return jnp.where(usable, listed, blocks_count)


def ring_of(mesh):
    chips = [devices[0] for devices in mesh.devices.reshape(-1, mesh.shape["shard"])[0].reshape(-1, 2)]
    count = len(chips)
    at = [getattr(chip, "coords", None) for chip in chips]
    if any(c is None for c in at):
        return tuple(range(count))
    near = lambda i, j: sum(abs(p - q) for p, q in zip(at[i], at[j])) == 1

    def grow(path):
        if len(path) == count:
            return path if near(path[-1], path[0]) else None
        for chip in range(count):
            if chip not in path and near(path[-1], chip):
                found = grow(path + [chip])
                if found:
                    return found
        return None

    return tuple(grow([0]) or range(count))


class Ring:
    def __init__(self, order):
        self.order = order
        self.count = len(order)
        self.far = self.count // 2
        self.stages = [[(0, 0), (0, 1)]]
        for k in range(1, self.far):
            self.stages.append([(k, 0), (self.count - k, 0), (k, 1), (self.count - k, 1)])
        self.stages.append([(self.far, 0), (self.far, 1)])
        self.pieces = [piece for stage in self.stages for piece in stage]

    def hop(self, table, by):
        pairs = [
            (2 * self.order[i] + core, 2 * self.order[(i + by) % self.count] + core)
            for i in range(self.count)
            for core in range(2)
        ]
        return lax.ppermute(table, "shard", pairs)

    def swap(self, table):
        return lax.ppermute(table, "shard", [(s, s ^ 1) for s in range(2 * self.count)])

    def sources(self):
        me = lax.axis_index("shard")
        order = jnp.array(self.order, jnp.int32)
        chip, core = me // 2, me % 2
        place = jnp.sum(jnp.where(order == chip, jnp.arange(self.count, dtype=jnp.int32), 0))
        ahead = jnp.array([k for k, _ in self.pieces], jnp.int32)
        other = jnp.array([e for _, e in self.pieces], jnp.int32)
        wanted = (place + ahead) % self.count
        found = jnp.sum(
            jnp.where(wanted[:, None] == jnp.arange(self.count, dtype=jnp.int32)[None], order[None], 0), axis=1
        )
        return 2 * found + jnp.bitwise_xor(core, other)

    def gather(self, table, use, ready):
        tie = lax.optimization_barrier
        half = table.shape[0] // 2
        used = []
        behind = ahead = table
        stages = [[table, self.swap(table)]]
        for k in range(1, self.far + 1):
            if k < self.far:
                ahead, behind = tie((self.hop(ahead, -1), self.hop(behind, 1)))
            else:
                ahead, behind = tie((self.hop(ahead[:half], -1), self.hop(behind[half:], 1)))
            if k == 2:
                ahead, behind, ready = tie((ahead, behind, ready))
            if k >= 2:
                used = used + [use(k - 2, stages[k - 2], ready)]
                ahead, behind, used = tie((ahead, behind, used))
            if k < self.far:
                stages.append([ahead, behind, self.swap(ahead), self.swap(behind)])
        both = jnp.concatenate([ahead, behind], axis=0)
        stages.append([both, self.swap(both)])
        return used + [use(i, stages[i], ready) for i in range(len(used), len(stages))], ahead

    def scatter_order(self):
        n, far = self.count, self.far
        return [far] + [k for near in range(far - 1, 0, -1) for k in (near, n - near)] + [0]

    def scatter_sum(self, own, other, release, finish):
        low = lambda t: t.astype(BF)
        n, far = self.count, self.far
        swapped = {k: self.swap(other[k]) for k in self.scatter_order()}
        own = {k: own[k].astype(F32) + swapped[k].astype(F32) for k in own}
        half = own[far].shape[0] // 2
        start = release(low(own[far]))
        up, down = self.hop(start[:half], 1), self.hop(start[half:], -1)
        blank = jnp.zeros(up.shape, F32)
        up = jnp.concatenate([up.astype(F32), blank], axis=0)
        down = jnp.concatenate([blank, down.astype(F32)], axis=0)
        for k in range(far - 1, 0, -1):
            up, down = low(own[k] + up), low(own[n - k] + down)
            if k == 1:
                up = finish(up)
            up, down = lax.optimization_barrier((up, down))
            up, down = self.hop(up, 1).astype(F32), self.hop(down, -1).astype(F32)
        return own[0] + up + down


def project_kernel(count, *refs):
    tokens, (seg_ref, w_ref, bias_ref, norm_ref), outs = refs[:count], refs[count : count + 4], refs[count + 4 :]
    n_ref, k_ref, kv_ref, q_ref, kt_ref, vt_ref = outs
    for i, tok_ref in enumerate(tokens):
        length = tok_ref.shape[0]
        tiles = length // 128
        cut = slice(i * length, (i + 1) * length)
        normal, _ = normalize(tok_ref[...].astype(F32))
        normed = (normal * norm_ref[0:1, :] + norm_ref[1:2, :]).astype(BF)
        n_ref[cut] = normed
        out = dot_nn(normed, w_ref[...]) + bias_ref[0:1, :]
        out = out.astype(BF).astype(F32)
        pair = out[:, :128]
        lane = lanes_of(pair.shape)
        seg = seg_ref[i : i + 1, :].astype(F32)
        apart = jnp.broadcast_to(seg, (128, length)).T != (lane - DH).astype(F32)
        extra = jnp.where((lane < DH + 8) & apart, FAR, 0.0)
        kv_ref[cut] = pair.astype(BF)
        k_ref[cut] = jnp.where(lane < DH, pair, extra).astype(BF)
        flat = pair.T
        query = out[:, 128:].T * (1.0 / math.sqrt(DH))
        for tile in range(tiles):
            across = slice(tile * 128, (tile + 1) * 128)
            row = lax.broadcasted_iota(jnp.int32, (128, 128), 0)
            same = jnp.broadcast_to(seg[:, across], (128, 128)) == (row - DH).astype(F32)
            hot = jnp.where((row < DH + 8) & same, 1.0, 0.0)
            q_ref[i * tiles + tile] = jnp.where(row < DH, query[:, across], hot).astype(BF)
            both = flat[:, across]
            turned = pltpu.roll(both, DH, 1)
            left = lanes_of(both.shape) < DH
            for block, twice in enumerate((jnp.where(left, both, turned), jnp.where(left, turned, both))):
                at = (i * tiles + tile) * 2 + block
                kt_ref[at] = twice[:DH].astype(BF)
                vt_ref[at] = twice[DH:].astype(BF)


def project(pieces, segs, weight, bias, norm_rows):
    length, width = pieces[0].shape
    total = length * len(pieces)
    table = jax.ShapeDtypeStruct((total, 128), BF)
    turned = jax.ShapeDtypeStruct((total // BLK, DH, 128), BF)
    return pl.pallas_call(
        functools.partial(project_kernel, len(pieces)),
        out_shape=[
            jax.ShapeDtypeStruct((total, width), BF),
            table,
            table,
            jax.ShapeDtypeStruct((total // 128, 128, 128), BF),
            turned,
            turned,
        ],
        compiler_params=params(),
        name="project",
    )(*pieces, segs, weight, bias, norm_rows)


def load_tables(pairs, sem):
    copies = []
    for sources, dst in pairs:
        start = 0
        for src in sources:
            count = src.shape[0]
            place = sem.at[len(copies)]
            copies.append(pltpu.make_async_copy(src, dst.at[pl.ds(start, count)], place))
            start += count
    for copy in copies:
        copy.start()
    for copy in copies:
        copy.wait()


def null_keys():
    lane = lanes_of((BLK, 128))
    return jnp.where((lane >= DH) & (lane < DH + 8), FAR, 0.0).astype(BF)


def blocks_of(idx_ref, place_ref, block):
    return [place_ref[idx_ref[block * SLOTS + slot]] for slot in range(SLOTS)]


def rows_of(blocks, ref):
    return jnp.concatenate([ref[pl.ds(pl.multiple_of(b * BLK, BLK), BLK), :] for b in blocks], axis=0)


def turned_of(blocks, ref):
    left = lanes_of((DH, 128)) < DH
    pairs = [jnp.where(left, ref[one], ref[two]) for one, two in zip(blocks[::2], blocks[1::2])]
    return jnp.concatenate(pairs, axis=1)


def halves(table):
    left = lanes_of(table.shape) < DH
    zero = jnp.zeros_like(table)
    return jnp.where(left, table, zero), jnp.where(left, zero, table)


def chances_of(low, high, query, k_ref):
    keys = jnp.concatenate([rows_of(low, k_ref), rows_of(high, k_ref)], axis=1)
    scores = dot_nn(keys, jnp.concatenate(halves(query), axis=0))
    raised = jnp.exp(scores - jnp.max(scores, axis=0, keepdims=True))
    return raised * (1.0 / jnp.sum(raised, axis=0, keepdims=True))


def attend_kernel(parts, idx_ref, src_ref, place_ref, *refs):
    tables, (o_ref, k_ref, q_ref, vt_ref, sem) = refs[: 3 * parts], refs[3 * parts :]
    load_tables(
        [(tables[i * parts : (i + 1) * parts], dst) for i, dst in enumerate((k_ref, q_ref, vt_ref))],
        sem,
    )
    rows = k_ref.shape[0] - BLK
    k_ref[rows:] = null_keys()
    vt_ref[rows // BLK] = jnp.zeros((DH, 128), BF)
    owners, _, count = o_ref.shape
    tiles = count // 128
    left = lanes_of((DH, 128)) < DH

    def step(piece, carry):
        owner = src_ref[piece]
        for tile in range(tiles):
            block = (owner * tiles + tile) * 2
            low, high = blocks_of(idx_ref, place_ref, block), blocks_of(idx_ref, place_ref, block + 1)
            chances = chances_of(low, high, q_ref[piece * tiles + tile], k_ref).astype(BF)
            values = jnp.concatenate([turned_of(low, vt_ref), turned_of(high, vt_ref)], axis=0)
            out = dot_nn(values, chances)
            o_ref[owner, :, tile * 128 : (tile + 1) * 128] = jnp.where(left, out[:DH], out[DH:]).astype(BF)
        return carry

    lax.fori_loop(0, owners, step, 0)


def attend(scalars, tables, owners):
    parts = len(tables[0])
    rows = sum(t.shape[0] for t in tables[0])
    anywhere = pl.BlockSpec(memory_space=pl.ANY)
    flat = [t for table in tables for t in table]
    return pl.pallas_call(
        functools.partial(attend_kernel, parts),
        in_specs=[pl.BlockSpec(memory_space=pltpu.SMEM)] * 3 + [anywhere] * len(flat),
        out_specs=pl.BlockSpec(memory_space=pltpu.VMEM),
        out_shape=jax.ShapeDtypeStruct((owners, DH, rows // owners), BF),
        scratch_shapes=[
            pltpu.VMEM((rows + BLK, 128), BF),
            pltpu.VMEM((rows // 128, 128, 128), BF),
            pltpu.VMEM((rows // BLK + 1, DH, 128), BF),
            pltpu.SemaphoreType.DMA((len(flat),)),
        ],
        compiler_params=params(),
        name="attend",
    )(*scalars, *flat)


def attend_back_kernel(parts, idx_ref, src_ref, place_ref, *refs):
    tables, (d_ref, k_ref, kv_ref, q_ref, kt_ref, g_ref, acc_ref, dq_ref, sem) = (
        refs[: 4 * parts + 1],
        refs[4 * parts + 1 :],
    )
    load_tables(
        [
            (tables[i * parts : (i + 1) * parts], dst)
            for i, dst in enumerate((k_ref, kv_ref, q_ref, kt_ref))
        ]
        + [(tables[4 * parts :], g_ref)],
        sem,
    )
    rows = k_ref.shape[0] - BLK
    k_ref[rows:] = null_keys()
    kv_ref[rows:] = jnp.zeros((BLK, 128), BF)
    kt_ref[rows // BLK] = jnp.zeros((DH, 128), BF)
    acc_ref[...] = jnp.zeros_like(acc_ref)
    owners, _, count = g_ref.shape
    tiles = count // 128
    left = lanes_of((DH, 128)) < DH
    zero = jnp.zeros((DH, 128), BF)

    def step(piece, carry):
        owner = src_ref[piece]
        for tile in range(tiles):
            block = (owner * tiles + tile) * 2
            low, high = blocks_of(idx_ref, place_ref, block), blocks_of(idx_ref, place_ref, block + 1)
            query = q_ref[piece * tiles + tile]
            chances = chances_of(low, high, query, k_ref)
            grad_low, grad_high = halves(g_ref[owner, :, tile * 128 : (tile + 1) * 128])
            values = jnp.concatenate([rows_of(low, kv_ref), rows_of(high, kv_ref)], axis=1)
            grad_chances = dot_nn(values, jnp.concatenate([zero, grad_low, zero, grad_high], axis=0))
            inner = jnp.sum(chances * grad_chances, axis=0, keepdims=True)
            grad_scores = (chances * (grad_chances - inner)).astype(BF)
            query_low, query_high = halves(query[:DH])
            right = jnp.concatenate(
                [
                    jnp.concatenate([query_low, zero], axis=1),
                    jnp.concatenate([zero, grad_low], axis=1),
                    jnp.concatenate([query_high, zero], axis=1),
                    jnp.concatenate([zero, grad_high], axis=1),
                ],
                axis=0,
            )
            adds = dot_nt(jnp.concatenate([grad_scores, chances.astype(BF)], axis=1), right)
            keys = jnp.concatenate([turned_of(low, kt_ref), turned_of(high, kt_ref)], axis=0)
            grad_query = dot_nn(keys, grad_scores)
            dq_ref[piece * tiles + tile] = jnp.where(left, grad_query[:DH], grad_query[DH:]) * (
                1.0 / math.sqrt(DH)
            )
            for side, blocks in enumerate((low, high)):
                for slot, b in enumerate(blocks):
                    at = pl.ds(pl.multiple_of(b * BLK, BLK), BLK)
                    acc_ref[at, :] += adds[slot * BLK : (slot + 1) * BLK, side * 128 : (side + 1) * 128]
        return carry

    lax.fori_loop(0, owners, step, 0)

    def finish(i, carry):
        at = pl.ds(pl.multiple_of(i * 128, 128), 128)
        d_ref[at, 0:128] = acc_ref[at, :].astype(BF)
        tile = jnp.concatenate([dq_ref[i], jnp.zeros((DH, 128), F32)], axis=0)
        d_ref[at, 128:256] = tile.T.astype(BF)
        return carry

    lax.fori_loop(0, rows // 128, finish, 0, unroll=4)


def attend_back(scalars, tables, grads):
    parts = len(tables[0])
    rows = sum(t.shape[0] for t in tables[0])
    anywhere = pl.BlockSpec(memory_space=pl.ANY)
    flat = [t for table in tables for t in table] + [grads]
    return pl.pallas_call(
        functools.partial(attend_back_kernel, parts),
        in_specs=[pl.BlockSpec(memory_space=pltpu.SMEM)] * 3 + [anywhere] * len(flat),
        out_specs=pl.BlockSpec(memory_space=pltpu.VMEM),
        out_shape=jax.ShapeDtypeStruct((rows, 256), BF),
        scratch_shapes=[
            pltpu.VMEM((rows + BLK, 128), BF),
            pltpu.VMEM((rows + BLK, 128), BF),
            pltpu.VMEM((rows // 128, 128, 128), BF),
            pltpu.VMEM((rows // BLK + 1, DH, 128), BF),
            pltpu.VMEM(grads.shape, BF),
            pltpu.VMEM((rows + BLK, 128), F32),
            pltpu.VMEM((rows // 128, DH, 128), F32),
            pltpu.SemaphoreType.DMA((len(flat),)),
        ],
        compiler_params=params(),
        name="attend_back",
    )(*scalars, *flat)


def out_kernel(att_ref, tok_ref, w_ref, vec_ref, mid_ref, n2_ref):
    width = tok_ref.shape[1]
    mid = (
        tok_ref[...].astype(F32)
        + dot_tn(att_ref[...].reshape(width, -1), w_ref[...].reshape(width, width))
        + vec_ref[0:1, :]
    )
    mid_ref[...] = mid
    normal, _ = normalize(mid)
    n2_ref[...] = (normal * vec_ref[1:2, :] + vec_ref[2:3, :]).astype(BF)


def whole(shape):
    return pl.BlockSpec(shape, lambda c: (0,) * len(shape))


def out_rows(weights):
    owners, rows, width = weights.shape
    own = width // owners
    return pl.BlockSpec((owners, own, width), lambda c: (0, rows // own - 1, 0))


def project_out(attended, tokens, weights, vectors):
    shape = tokens.shape
    return pl.pallas_call(
        out_kernel,
        grid=(1,),
        in_specs=[whole(attended.shape), whole(shape), out_rows(weights), whole(vectors.shape)],
        out_specs=[whole(shape)] * 2,
        out_shape=[jax.ShapeDtypeStruct(shape, F32), jax.ShapeDtypeStruct(shape, BF)],
        compiler_params=params("arbitrary"),
        name="project_out",
    )(attended, tokens, weights, vectors)


def feed_kernel(n2_ref, cot_ref, down_ref, up_ref, vec_ref, out_ref, gn_ref, hid_ref, pre_ref, gb_ref, acc_ref, acc_gn):
    chunk = pl.program_id(0)
    width = n2_ref.shape[1]
    w_up = up_ref[...].reshape(width, -1)
    w_down = down_ref[...].reshape(-1, width)
    pre = dot_nn(n2_ref[...], w_up) + vec_ref[pl.ds(4 + chunk, 1), :]
    root = math.sqrt(2.0 / math.pi)
    square = pre * pre
    bent = jnp.tanh(root * (pre + 0.044715 * (pre * square)))
    hidden = (0.5 * pre * (1.0 + bent)).astype(BF)
    slope = 0.5 * (1.0 + bent) + 0.5 * pre * (1.0 - bent * bent) * (
        root * (1.0 + (3 * 0.044715) * square)
    )
    grad_pre = (slope * dot_nt(cot_ref[...], w_down)).astype(BF)
    hid_ref[...] = hidden
    pre_ref[...] = grad_pre
    gb_ref[pl.ds(chunk, 1), :] = jnp.sum(grad_pre.astype(F32), axis=0, keepdims=True)
    more = dot_nn(hidden, w_down)
    grad_more = dot_nt(grad_pre, w_up)

    @pl.when(chunk == 0)
    def _():
        acc_ref[...] = more
        acc_gn[...] = grad_more

    @pl.when(chunk > 0)
    def _():
        out_ref[...] = (acc_ref[...] + more).astype(out_ref.dtype)
        gn_ref[...] = (acc_gn[...] + grad_more).astype(gn_ref.dtype)


def layout_of(weights):
    owners, rows, width = weights.shape
    own = width // owners
    units = (rows - own) // 2
    chunks = units // own
    return owners, own, width, units, chunks


def feed(normed, cotangent, weights, vectors, kind):
    owners, own, width, units, chunks = layout_of(weights)
    assert chunks == 2
    count = normed.shape[0]
    first_up = units // own
    column = pl.BlockSpec((count, width), lambda c: (0, c))
    wide = jax.ShapeDtypeStruct((count, chunks * width), BF)
    return pl.pallas_call(
        feed_kernel,
        grid=(chunks,),
        in_specs=[
            whole(normed.shape),
            whole(cotangent.shape),
            pl.BlockSpec((owners // chunks, units, width), lambda c: (c, 0, 0)),
            pl.BlockSpec((owners, own, width), lambda c: (0, first_up + c, 0)),
            whole(vectors.shape),
        ],
        out_specs=[whole((count, width))] * 2 + [column, column, whole((8, width))],
        out_shape=[
            jax.ShapeDtypeStruct((count, width), kind),
            jax.ShapeDtypeStruct((count, width), kind),
            wide,
            wide,
            jax.ShapeDtypeStruct((8, width), F32),
        ],
        scratch_shapes=[pltpu.VMEM((count, width), F32), pltpu.VMEM((count, width), F32)],
        compiler_params=params("arbitrary"),
        name="feed",
    )(normed, cotangent, weights, weights, vectors)


def feed_grads_kernel(na_ref, nb_ref, ca_ref, cb_ref, ha_ref, hb_ref, pa_ref, pb_ref, grads_hbm, gd_buf, gu_buf, sem):
    chunk = pl.program_id(0)
    down_block, down_rows = gd_buf.shape[1:3]
    up_rows = gu_buf.shape[2]
    down = dot_tn(ha_ref[...], ca_ref[...]) + dot_tn(hb_ref[...], cb_ref[...])
    gd_buf[chunk] = down.astype(BF).reshape(gd_buf.shape[1:])
    copy_down = lambda c: pltpu.make_async_copy(
        gd_buf.at[c],
        grads_hbm.at[pl.ds(c * down_block, down_block), pl.ds(0, down_rows)],
        sem.at[0, c],
    )
    copy_up = lambda c: pltpu.make_async_copy(
        gu_buf.at[c],
        grads_hbm.at[:, pl.ds(down_rows + c * up_rows, up_rows)],
        sem.at[1, c],
    )
    copy_down(chunk).start()
    up = dot_tn(na_ref[...], pa_ref[...]) + dot_tn(nb_ref[...], pb_ref[...])
    gu_buf[chunk] = up.astype(BF).reshape(gu_buf.shape[1:])
    copy_up(chunk).start()

    @pl.when(chunk == 1)
    def _():
        for c in range(2):
            copy_down(c).wait()
            copy_up(c).wait()


def feed_grads(own_part, other_part, weights):
    owners, own, width, units, chunks = layout_of(weights)
    count = own_part[0].shape[0]
    column = pl.BlockSpec((count, width), lambda c: (0, c))
    inputs = [t for both in zip(own_part, other_part) for t in both]
    return pl.pallas_call(
        feed_grads_kernel,
        grid=(chunks,),
        in_specs=[whole((count, width))] * 4 + [column] * 4,
        out_specs=pl.BlockSpec(memory_space=pl.ANY),
        out_shape=jax.ShapeDtypeStruct(weights.shape, BF),
        scratch_shapes=[
            pltpu.VMEM((chunks, owners // chunks, units, width), BF),
            pltpu.VMEM((chunks, owners, own, width), BF),
            pltpu.SemaphoreType.DMA((2, chunks)),
        ],
        compiler_params=params("arbitrary"),
        name="feed_grads",
    )(*inputs)


def out_back_kernel(
    mid_ref, gn_ref, other_ref, cot_ref, att_ref, w_ref, vec_ref, _, gm_ref, ga_ref, gv_ref, grads_hbm, buf, sem
):
    width = mid_ref.shape[1]
    rows = grads_hbm.shape[1]
    normal, scale = normalize(mid_ref[...])
    grad = gn_ref[...] + other_ref[...].astype(F32)
    cot = cot_ref[...].astype(F32)
    grad_mid = cot + norm_backward(grad, normal, scale, vec_ref[1:2, :])
    gm_ref[...] = grad_mid
    branch = grad_mid.astype(BF)
    ga_ref[...] = dot_nt(w_ref[...].reshape(width, width), branch).astype(BF).reshape(ga_ref.shape)
    buf[...] = dot_nn(att_ref[...].reshape(width, -1), branch).astype(BF).reshape(buf.shape)
    copy = pltpu.make_async_copy(buf, grads_hbm.at[:, pl.ds(rows - buf.shape[1], buf.shape[1])], sem)
    copy.start()
    gv_ref[...] = jnp.zeros_like(gv_ref)
    gv_ref[0:1, :] = jnp.sum(branch.astype(F32), axis=0, keepdims=True)
    gv_ref[1:2, :] = jnp.sum(grad * normal, axis=0, keepdims=True)
    gv_ref[2:3, :] = jnp.sum(grad, axis=0, keepdims=True)
    gv_ref[3:4, :] = jnp.sum(cot, axis=0, keepdims=True)
    copy.wait()


def project_out_back(mid, grad, other, cotangent, attended, weights, vectors, grads):
    owners, own, width, units, chunks = layout_of(weights)
    shape = mid.shape
    packed = attended.shape
    anywhere = pl.BlockSpec(memory_space=pl.ANY)
    return pl.pallas_call(
        out_back_kernel,
        grid=(1,),
        in_specs=[whole(shape)] * 4 + [whole(packed), out_rows(weights), whole(vectors.shape), anywhere],
        out_specs=[whole(shape), whole(packed), whole((8, width)), anywhere],
        out_shape=[
            jax.ShapeDtypeStruct(shape, F32),
            jax.ShapeDtypeStruct(packed, BF),
            jax.ShapeDtypeStruct((8, width), F32),
            jax.ShapeDtypeStruct(grads.shape, BF),
        ],
        scratch_shapes=[pltpu.VMEM((owners, own, width), BF), pltpu.SemaphoreType.DMA],
        input_output_aliases={7: 3},
        compiler_params=params("arbitrary"),
        name="project_out_back",
    )(mid, grad, other, cotangent, attended, weights, vectors, grads)


def shares_kernel(starts, d_ref, w_ref, *outs):
    weight = w_ref[...]
    for start, out_ref in zip(starts, outs):
        out_ref[...] = dot_nt(d_ref[start : start + out_ref.shape[0], :], weight).astype(BF)


def head_shares(grad_table, weight, starts, count):
    width = weight.shape[0]
    return pl.pallas_call(
        functools.partial(shares_kernel, starts),
        out_shape=[jax.ShapeDtypeStruct((count, width), BF)] * len(starts),
        compiler_params=params(),
        name="head_shares",
    )(grad_table, weight)


def last_kernel(tok_ref, gn_ref, gm_ref, norm_ref, out_ref):
    normal, scale = normalize(tok_ref[...].astype(F32))
    grad = norm_backward(gn_ref[...], normal, scale, norm_ref[0:1, :])
    out_ref[...] = (gm_ref[...] + grad).astype(BF)


def last(tokens, grad_normed, grad_middle, norm_rows):
    return pl.pallas_call(
        last_kernel,
        out_shape=jax.ShapeDtypeStruct(tokens.shape, BF),
        compiler_params=params(),
        name="last",
    )(tokens, grad_normed, grad_middle, norm_rows)


def exchange(table):
    return lax.all_to_all(table, "shard", split_axis=0, concat_axis=0, tiled=True)


def trade(table):
    reps = lax.axis_size("rep")
    return lax.ppermute(table, "rep", [(r, r ^ 1) for r in range(reps)])


def over_alike(table):
    reps = lax.axis_size("rep")
    if reps == 2:
        return table
    groups = [list(range(first, reps, 2)) for first in range(2)]
    return lax.psum(table, "rep", axis_index_groups=groups)


def local(
    ring,
    tokens,
    cotangent,
    seg_ids,
    random_blocks,
    global_blocks,
    ln1_gain,
    ln1_bias,
    w_query,
    b_query,
    w_key,
    w_value,
    b_value,
    w_out,
    b_out,
    ln2_gain,
    ln2_bias,
    w_up,
    b_up,
    w_down,
    b_down,
):
    tokens, cotangent, seg_row = tokens[0], cotangent[0], seg_ids[0]
    count, width = tokens.shape
    owners = lax.axis_size("shard")
    own = width // owners
    hidden = w_up.shape[1]
    units = hidden // owners // 2
    half = lax.axis_index("rep") % 2

    tiles = jnp.concatenate(
        [w.reshape(own, owners, DH) for w in (w_key, w_value, w_query)], axis=2
    ).transpose(1, 0, 2)
    small = jnp.concatenate([b_out, ln2_gain, ln2_bias, b_down, ln1_gain, ln1_bias, b_up])
    small = jnp.pad(small, (0, own * DH - small.shape[0])).reshape(1, own, DH)
    sent = jnp.concatenate([tiles, jnp.broadcast_to(small, (owners, own, DH))], axis=2)
    got = exchange(sent)
    weight = jnp.pad(got[:, :, : 3 * DH], ((0, 0), (0, 0), (0, DH))).reshape(width, 4 * DH)
    rows = got[:, :, 3 * DH :].reshape(owners, own * DH)[:, : 6 * own + hidden // owners]
    rows = rows.astype(F32)
    fixed = rows[:, : 6 * own].reshape(owners, 6, own).transpose(1, 0, 2).reshape(6, width)
    up_bias = lax.dynamic_slice_in_dim(rows[:, 6 * own :], half * units, units, axis=1)
    vectors = jnp.concatenate([fixed[:4], up_bias.reshape(2, width), jnp.zeros((2, width), F32)], axis=0)
    norm_rows = jnp.pad(fixed[4:6], ((0, 6), (0, 0)))
    zero = jnp.zeros((DH,), F32)
    bias = jnp.concatenate([zero, b_value.astype(F32), b_query.astype(F32), zero])
    bias = jnp.broadcast_to(bias[None], (8, 4 * DH))

    up_half = lax.dynamic_index_in_dim(w_up.reshape(own, owners, 2, units), half, 2, keepdims=False)
    mine = jnp.concatenate(
        [
            lax.dynamic_slice_in_dim(w_down, half * units, units, axis=0),
            up_half.reshape(own, 2, width).transpose(1, 0, 2).reshape(2 * own, width),
            w_out,
        ],
        axis=0,
    )
    other_cotangent = trade(cotangent)

    per = count // BLK
    sources = ring.sources()
    idx = key_blocks(random_blocks[0, 0], global_blocks[0])
    position = jnp.arange(owners, dtype=jnp.int32)
    piece_of = jnp.sum(jnp.where(sources[None] == position[:, None], position[None], 0), axis=1)
    place = piece_of[:, None] * per + jnp.arange(per, dtype=jnp.int32)[None]
    place = jnp.concatenate([place.reshape(-1), jnp.full((1,), owners * per, jnp.int32)])
    scalars = (idx.reshape(-1), sources, place)
    segs = seg_row.reshape(owners, count)[sources]

    def use(stage, pieces, ready):
        first = sum(len(earlier) for earlier in ring.stages[:stage])
        segs_here = jnp.pad(segs[first : first + len(pieces)], ((0, 8 - len(pieces)), (0, 0)))
        return project(pieces, segs_here, *ready)

    projected, late = ring.gather(tokens, use, (weight, bias, norm_rows))
    mine, _ = lax.optimization_barrier((mine, late))
    weights = lax.all_gather(mine, "shard", axis=0)
    projected, other_cotangent = lax.optimization_barrier((projected, other_cotangent))
    table = lambda *which: [[stage[i] for stage in projected] for i in which]
    attended = exchange(attend(scalars, table(1, 3, 5), owners))
    mid, normed_two = project_out(attended, tokens, weights, vectors)
    other_normed = trade(normed_two)
    more, grad_two, hid, grad_pre, bias_one = feed(normed_two, cotangent, weights, vectors, F32)
    other_normed, grad_two = lax.optimization_barrier((other_normed, grad_two))
    other_more, other_grad, other_hid, other_pre, bias_two = feed(
        other_normed, other_cotangent, weights, vectors, BF
    )
    other_grad = trade(other_grad)
    other_more = trade(other_more)
    grads = feed_grads(
        (normed_two, cotangent, hid, grad_pre),
        (other_normed, other_cotangent, other_hid, other_pre),
        weights,
    )
    grad_middle, grad_attended, grad_rows, grads = project_out_back(
        mid, grad_two, other_grad, cotangent, attended, weights, vectors, grads
    )
    layer_out = (mid + more + other_more.astype(F32) + fixed[3][None]).astype(BF)
    shares = lax.psum_scatter(
        grads.reshape(-1, width), "shard", scatter_dimension=0, tiled=True
    )
    grad_table = attend_back(scalars, table(1, 2, 3, 4), exchange(grad_attended))
    at = {piece: i * count for i, piece in enumerate(ring.pieces)}
    order = ring.scatter_order()
    other_shares = head_shares(grad_table, weight, [at[k, 1] for k in order], count)
    table_later, _ = lax.optimization_barrier((grad_table, other_shares))
    own_shares = head_shares(table_later, weight, [at[k, 0] for k in order], count)
    results = []

    def release(first):
        first, table = lax.optimization_barrier((first, grad_table))
        results.append(weight_grads(table))
        return first

    def weight_grads(table):
        grad_weight, done = 0.0, 0
        for stage in projected:
            normed = stage[0]
            grad_weight = grad_weight + dot_tn(normed, table[done : done + normed.shape[0]])
            done += normed.shape[0]
        return finish_weights(grad_weight, jnp.sum(table.astype(F32), axis=0, keepdims=True))

    def finish(rows):
        tied = lax.optimization_barrier((rows, results[0]))
        results[0] = tied[1]
        return tied[0]

    def finish_weights(grad_weight, grad_bias):
        used = weight.astype(F32)[:, : 3 * DH]
        sums = grad_bias[0:1, : 3 * DH]
        spread = grad_weight[:, : 3 * DH] - fixed[5][:, None] * sums
        grad_gain = jnp.sum(used * spread, axis=1) / fixed[4]
        grad_shift = jnp.sum(used * sums, axis=1)
        lines = jnp.concatenate([grad_rows[:4], grad_gain[None], grad_shift[None]], axis=0)
        lines = lines.reshape(6, owners, own).transpose(1, 0, 2).reshape(owners, 6 * own)
        up_lines = (bias_one[:2] + bias_two[:2]).reshape(owners, units)
        lines = jnp.concatenate([lines, up_lines], axis=1)
        length = lines.shape[1]
        lines = jnp.pad(lines, ((0, 0), (0, own * DH - length))).reshape(owners, own, DH)
        back = jnp.concatenate(
            [grad_weight[:, : 3 * DH].reshape(owners, own, 3 * DH), lines], axis=2
        ).astype(BF)
        back = exchange(back)
        back_sum = jnp.sum(back[:, :, 3 * DH :].astype(F32), axis=0).reshape(own * DH)[:length]
        heads = over_alike(back[:, :, : 3 * DH])
        heads = heads.astype(F32) + trade(heads).astype(F32)
        heads = heads.transpose(1, 2, 0).reshape(own, 3, DH, owners).transpose(1, 0, 3, 2)
        heads = heads.reshape(3, own, width)
        tail = jnp.concatenate([back_sum, grad_bias[0, 2 * DH : 3 * DH], grad_bias[0, DH : 2 * DH]])
        tail = over_alike(tail.astype(BF))
        tail_other = trade(tail).astype(F32)
        tail = tail.astype(F32)
        total = tail + tail_other
        piece = lambda i: total[i * own : (i + 1) * own]

        def in_order(here, there, axis):
            both = [jnp.where(half == 0, here, there), jnp.where(half == 0, there, here)]
            return jnp.stack(both, axis=axis)

        grad_up_bias = in_order(tail[6 * own : length], tail_other[6 * own : length], 0).reshape(-1)
        ours = over_alike(shares)
        theirs = trade(ours)
        ours, theirs = ours.astype(F32), theirs.astype(F32)
        grad_down = in_order(ours[:units], theirs[:units], 0).reshape(2 * units, width)
        up_of = lambda t: t[units : 2 * units].reshape(2, own, width).transpose(1, 0, 2).reshape(
            own, owners, units
        )
        grad_up = in_order(up_of(ours), up_of(theirs), 2).reshape(own, hidden)
        grad_out = ours[2 * units :] + theirs[2 * units :]
        return (
            piece(4),
            piece(5),
            heads[2],
            total[length : length + DH],
            heads[0],
            heads[1],
            total[length + DH :],
            grad_out,
            piece(0),
            piece(1),
            piece(2),
            grad_up,
            grad_up_bias,
            grad_down,
            piece(3),
        )

    grad_normed = ring.scatter_sum(
        dict(zip(order, own_shares)), dict(zip(order, other_shares)), release, finish
    )
    grad_tokens = last(tokens, grad_normed, grad_middle, norm_rows)
    return (layer_out[None], grad_tokens[None], *results[0])


def solution(mesh):
    rows = P("rep", "shard", None)
    one, two = P("shard"), P("shard", None)
    return jax.shard_map(
        functools.partial(local, Ring(ring_of(mesh))),
        mesh=mesh,
        in_specs=(
            rows, rows, P("rep", None), P("rep", "shard", None, None), P("rep", None),
            one, one, two, one, two, two, one, two, one, one, one, two, one, two, one,
        ),
        out_specs=(
            rows, rows, one, one, two, one, two, two, one, two, one, one, one, two, one, two, one,
        ),
        check_vma=False,
    )
```

```python
import functools
import math

import jax
import jax.numpy as jnp
from jax import lax
from jax.experimental import pallas as pl
from jax.experimental.pallas import tpu as pltpu
from jax.sharding import PartitionSpec as P

BLK = 64
DH = 64
SLOTS = 8
EPSILON = 1e-05
FAR = -1e20
GATE = 4
BF = jnp.bfloat16
F32 = jnp.float32
VMEM_LIMIT = 56 * 1024 * 1024


def dot_nn(left, right):
    return lax.dot_general(left, right, (((1,), (0,)), ((), ())), preferred_element_type=F32)


def dot_tn(left, right):
    return lax.dot_general(left, right, (((0,), (0,)), ((), ())), preferred_element_type=F32)


def dot_nt(left, right):
    return lax.dot_general(left, right, (((1,), (1,)), ((), ())), preferred_element_type=F32)


def params(*semantics):
    return pltpu.CompilerParams(
        dimension_semantics=semantics if semantics else None, vmem_limit_bytes=VMEM_LIMIT
    )


def lanes_of(shape):
    return lax.broadcasted_iota(jnp.int32, shape, len(shape) - 1)


def normalize(values):
    centre = jnp.mean(values, axis=-1, keepdims=True)
    centred = values - centre
    spread = jnp.mean(centred * centred, axis=-1, keepdims=True)
    scale = lax.rsqrt(spread + EPSILON)
    return centred * scale, scale


def norm_backward(grad, normal, scale, gain):
    scaled = grad * gain
    mean_one = jnp.mean(scaled, axis=-1, keepdims=True)
    mean_two = jnp.mean(scaled * normal, axis=-1, keepdims=True)
    return scale * (scaled - mean_one - normal * mean_two)


def key_blocks(random_heads, global_ids):
    blocks_count = random_heads.shape[0]
    position = jnp.arange(blocks_count, dtype=jnp.int32)
    window = jnp.stack([position - 1, position, position + 1], axis=1)
    global_all = jnp.broadcast_to(global_ids[None, :], (blocks_count, global_ids.shape[0]))
    listed = jnp.concatenate([window, random_heads, global_all], axis=1)
    slot_count = listed.shape[1]
    earlier = jnp.arange(slot_count)[:, None] > jnp.arange(slot_count)[None, :]
    repeated = jnp.any((listed[..., :, None] == listed[..., None, :]) & earlier, axis=-1)
    usable = (listed >= 0) & (listed < blocks_count) & jnp.logical_not(repeated)
    return jnp.where(usable, listed, blocks_count)


def ring_of(mesh):
    chips = [devices[0] for devices in mesh.devices.reshape(-1, mesh.shape["shard"])[0].reshape(-1, 2)]
    count = len(chips)
    at = [getattr(chip, "coords", None) for chip in chips]
    if any(c is None for c in at):
        return tuple(range(count))
    near = lambda i, j: sum(abs(p - q) for p, q in zip(at[i], at[j])) == 1

    def grow(path):
        if len(path) == count:
            return path if near(path[-1], path[0]) else None
        for chip in range(count):
            if chip not in path and near(path[-1], chip):
                found = grow(path + [chip])
                if found:
                    return found
        return None

    return tuple(grow([0]) or range(count))


class Ring:
    def __init__(self, order):
        self.order = order
        self.count = len(order)
        self.far = self.count // 2
        self.stages = [[(0, 0), (0, 1)]]
        for k in range(1, self.far):
            self.stages.append([(k, 0), (self.count - k, 0), (k, 1), (self.count - k, 1)])
        self.stages.append([(self.far, 0), (self.far, 1)])
        self.pieces = [piece for stage in self.stages for piece in stage]

    def hop(self, table, by):
        pairs = [
            (2 * self.order[i] + core, 2 * self.order[(i + by) % self.count] + core)
            for i in range(self.count)
            for core in range(2)
        ]
        return lax.ppermute(table, "shard", pairs)

    def swap(self, table):
        return lax.ppermute(table, "shard", [(s, s ^ 1) for s in range(2 * self.count)])

    def sources(self):
        me = lax.axis_index("shard")
        order = jnp.array(self.order, jnp.int32)
        chip, core = me // 2, me % 2
        place = jnp.sum(jnp.where(order == chip, jnp.arange(self.count, dtype=jnp.int32), 0))
        ahead = jnp.array([k for k, _ in self.pieces], jnp.int32)
        other = jnp.array([e for _, e in self.pieces], jnp.int32)
        wanted = (place + ahead) % self.count
        found = jnp.sum(
            jnp.where(wanted[:, None] == jnp.arange(self.count, dtype=jnp.int32)[None], order[None], 0), axis=1
        )
        return 2 * found + jnp.bitwise_xor(core, other)

    def gather(self, table, use, ready, gate, step):
        tie = lax.optimization_barrier
        half = table.shape[0] // 2
        used = []
        behind = ahead = table
        stages = [[table, self.swap(table)]]
        for k in range(1, self.far + 1):
            if k < self.far:
                ahead, behind = tie((self.hop(ahead, -1), self.hop(behind, 1)))
            else:
                ahead, behind = tie((self.hop(ahead[:half], -1), self.hop(behind[half:], 1)))
            if k == 2:
                ahead, behind, ready = tie((ahead, behind, ready))
            if k >= 2:
                used = used + [use(k - 2, stages[k - 2], ready)]
                ahead, behind, used = tie((ahead, behind, used))
            if k == step:
                ahead = gate(ahead)
            if k < self.far:
                stages.append([ahead, behind, self.swap(ahead), self.swap(behind)])
        both = jnp.concatenate([ahead, behind], axis=0)
        stages.append([both, self.swap(both)])
        return used + [use(i, stages[i], ready) for i in range(len(used), len(stages))]

    def scatter_order(self):
        n, far = self.count, self.far
        return [far] + [k for near in range(far - 1, 0, -1) for k in (near, n - near)] + [0]

    def scatter_sum(self, own, other, release, finish):
        n, far = self.count, self.far
        swapped = {k: self.swap(other[k]) for k in self.scatter_order()}
        first = (own[far].astype(F32) + swapped[far].astype(F32)).astype(BF)
        half = first.shape[0] // 2
        up, down = lax.optimization_barrier((self.hop(first[:half], 1), self.hop(first[half:], -1)))
        up = release(up)
        for k in range(far - 1, 0, -1):
            up, down = ring_add(own[k], swapped[k], up, own[n - k], swapped[n - k], down)
            up, down = lax.optimization_barrier((self.hop(up, 1), self.hop(down, -1)))
        up = finish(up)
        return own[0], swapped[0], up, down


def ring_add_kernel(own_up, swap_up, up, own_down, swap_down, down, out_up, out_down):
    length, came = own_up.shape[0], up.shape[0]
    for own, swap, more, out, start in (
        (own_up, swap_up, up, out_up, 0),
        (own_down, swap_down, down, out_down, length - came),
    ):
        for at in range(0, length, came):
            cut = slice(at, at + came)
            total = own[cut].astype(F32) + swap[cut].astype(F32)
            if at == start:
                total = total + more[...].astype(F32)
            out[cut] = total.astype(BF)


def ring_add(*tables):
    shape = jax.ShapeDtypeStruct(tables[0].shape, BF)
    return pl.pallas_call(
        ring_add_kernel, out_shape=[shape, shape], compiler_params=params(), name="ring_add"
    )(*tables)


def project_kernel(count, *refs):
    tokens, (seg_ref, w_ref, bias_ref, norm_ref), outs = refs[:count], refs[count : count + 4], refs[count + 4 :]
    n_ref, k_ref, kv_ref, q_ref, kt_ref, vt_ref = outs
    for i, tok_ref in enumerate(tokens):
        length = tok_ref.shape[0]
        tiles = length // 128
        cut = slice(i * length, (i + 1) * length)
        normal, _ = normalize(tok_ref[...].astype(F32))
        normed = (normal * norm_ref[0:1, :] + norm_ref[1:2, :]).astype(BF)
        n_ref[cut] = normed
        out = dot_nn(normed, w_ref[...]) + bias_ref[0:1, :]
        out = out.astype(BF).astype(F32)
        pair = out[:, :128]
        lane = lanes_of(pair.shape)
        seg = seg_ref[i : i + 1, :].astype(F32)
        apart = jnp.broadcast_to(seg, (128, length)).T != (lane - DH).astype(F32)
        extra = jnp.where((lane < DH + 8) & apart, FAR, 0.0)
        kv_ref[cut] = pair.astype(BF)
        k_ref[cut] = jnp.where(lane < DH, pair, extra).astype(BF)
        flat = pair.T
        query = out[:, 128:].T * (1.0 / math.sqrt(DH))
        for tile in range(tiles):
            across = slice(tile * 128, (tile + 1) * 128)
            row = lax.broadcasted_iota(jnp.int32, (128, 128), 0)
            same = jnp.broadcast_to(seg[:, across], (128, 128)) == (row - DH).astype(F32)
            hot = jnp.where((row < DH + 8) & same, 1.0, 0.0)
            q_ref[i * tiles + tile] = jnp.where(row < DH, query[:, across], hot).astype(BF)
            both = flat[:, across]
            turned = pltpu.roll(both, DH, 1)
            left = lanes_of(both.shape) < DH
            for block, twice in enumerate((jnp.where(left, both, turned), jnp.where(left, turned, both))):
                at = (i * tiles + tile) * 2 + block
                kt_ref[at] = twice[:DH].astype(BF)
                vt_ref[at] = twice[DH:].astype(BF)


def project(pieces, segs, weight, bias, norm_rows):
    length, width = pieces[0].shape
    total = length * len(pieces)
    table = jax.ShapeDtypeStruct((total, 128), BF)
    turned = jax.ShapeDtypeStruct((total // BLK, DH, 128), BF)
    return pl.pallas_call(
        functools.partial(project_kernel, len(pieces)),
        out_shape=[
            jax.ShapeDtypeStruct((total, width), BF),
            table,
            table,
            jax.ShapeDtypeStruct((total // 128, 128, 128), BF),
            turned,
            turned,
        ],
        compiler_params=params(),
        name="project",
    )(*pieces, segs, weight, bias, norm_rows)


def load_tables(pairs, sem):
    copies = []
    for sources, dst in pairs:
        start = 0
        for src in sources:
            count = src.shape[0]
            place = sem.at[len(copies)]
            copies.append(pltpu.make_async_copy(src, dst.at[pl.ds(start, count)], place))
            start += count
    for copy in copies:
        copy.start()
    for copy in copies:
        copy.wait()


def null_keys():
    lane = lanes_of((BLK, 128))
    return jnp.where((lane >= DH) & (lane < DH + 8), FAR, 0.0).astype(BF)


def blocks_of(idx_ref, place_ref, block):
    return [place_ref[idx_ref[block * SLOTS + slot]] for slot in range(SLOTS)]


def rows_of(blocks, ref):
    return jnp.concatenate([ref[pl.ds(pl.multiple_of(b * BLK, BLK), BLK), :] for b in blocks], axis=0)


def turned_of(blocks, ref):
    left = lanes_of((DH, 128)) < DH
    pairs = [jnp.where(left, ref[one], ref[two]) for one, two in zip(blocks[::2], blocks[1::2])]
    return jnp.concatenate(pairs, axis=1)


def halves(table):
    left = lanes_of(table.shape) < DH
    zero = jnp.zeros_like(table)
    return jnp.where(left, table, zero), jnp.where(left, zero, table)


def chances_of(low, high, query, k_ref):
    keys = jnp.concatenate([rows_of(low, k_ref), rows_of(high, k_ref)], axis=1)
    scores = dot_nn(keys, jnp.concatenate(halves(query), axis=0))
    raised = jnp.exp(scores - jnp.max(scores, axis=0, keepdims=True))
    return raised * (1.0 / jnp.sum(raised, axis=0, keepdims=True))


def attend_kernel(parts, idx_ref, src_ref, place_ref, *refs):
    tables, (o_ref, k_ref, q_ref, vt_ref, sem) = refs[: 3 * parts], refs[3 * parts :]
    load_tables(
        [(tables[i * parts : (i + 1) * parts], dst) for i, dst in enumerate((k_ref, q_ref, vt_ref))],
        sem,
    )
    rows = k_ref.shape[0] - BLK
    k_ref[rows:] = null_keys()
    vt_ref[rows // BLK] = jnp.zeros((DH, 128), BF)
    owners, _, count = o_ref.shape
    tiles = count // 128
    left = lanes_of((DH, 128)) < DH

    def step(piece, carry):
        owner = src_ref[piece]
        for tile in range(tiles):
            block = (owner * tiles + tile) * 2
            low, high = blocks_of(idx_ref, place_ref, block), blocks_of(idx_ref, place_ref, block + 1)
            chances = chances_of(low, high, q_ref[piece * tiles + tile], k_ref).astype(BF)
            values = jnp.concatenate([turned_of(low, vt_ref), turned_of(high, vt_ref)], axis=0)
            out = dot_nn(values, chances)
            o_ref[owner, :, tile * 128 : (tile + 1) * 128] = jnp.where(left, out[:DH], out[DH:]).astype(BF)
        return carry

    lax.fori_loop(0, owners, step, 0)


def attend(scalars, tables, owners):
    parts = len(tables[0])
    rows = sum(t.shape[0] for t in tables[0])
    anywhere = pl.BlockSpec(memory_space=pl.ANY)
    flat = [t for table in tables for t in table]
    return pl.pallas_call(
        functools.partial(attend_kernel, parts),
        in_specs=[pl.BlockSpec(memory_space=pltpu.SMEM)] * 3 + [anywhere] * len(flat),
        out_specs=pl.BlockSpec(memory_space=pltpu.VMEM),
        out_shape=jax.ShapeDtypeStruct((owners, DH, rows // owners), BF),
        scratch_shapes=[
            pltpu.VMEM((rows + BLK, 128), BF),
            pltpu.VMEM((rows // 128, 128, 128), BF),
            pltpu.VMEM((rows // BLK + 1, DH, 128), BF),
            pltpu.SemaphoreType.DMA((len(flat),)),
        ],
        compiler_params=params(),
        name="attend",
    )(*scalars, *flat)


def attend_back_kernel(parts, idx_ref, src_ref, place_ref, *refs):
    tables, (d_ref, k_ref, kv_ref, q_ref, kt_ref, g_ref, acc_ref, dq_ref, sem) = (
        refs[: 4 * parts + 1],
        refs[4 * parts + 1 :],
    )
    load_tables(
        [
            (tables[i * parts : (i + 1) * parts], dst)
            for i, dst in enumerate((k_ref, kv_ref, q_ref, kt_ref))
        ]
        + [(tables[4 * parts :], g_ref)],
        sem,
    )
    rows = k_ref.shape[0] - BLK
    k_ref[rows:] = null_keys()
    kv_ref[rows:] = jnp.zeros((BLK, 128), BF)
    kt_ref[rows // BLK] = jnp.zeros((DH, 128), BF)
    acc_ref[...] = jnp.zeros_like(acc_ref)
    owners, _, count = g_ref.shape
    tiles = count // 128
    left = lanes_of((DH, 128)) < DH
    zero = jnp.zeros((DH, 128), BF)

    def step(piece, carry):
        owner = src_ref[piece]
        for tile in range(tiles):
            block = (owner * tiles + tile) * 2
            low, high = blocks_of(idx_ref, place_ref, block), blocks_of(idx_ref, place_ref, block + 1)
            query = q_ref[piece * tiles + tile]
            chances = chances_of(low, high, query, k_ref)
            grad_low, grad_high = halves(g_ref[owner, :, tile * 128 : (tile + 1) * 128])
            values = jnp.concatenate([rows_of(low, kv_ref), rows_of(high, kv_ref)], axis=1)
            grad_chances = dot_nn(values, jnp.concatenate([zero, grad_low, zero, grad_high], axis=0))
            inner = jnp.sum(chances * grad_chances, axis=0, keepdims=True)
            grad_scores = (chances * (grad_chances - inner)).astype(BF)
            query_low, query_high = halves(query[:DH])
            right = jnp.concatenate(
                [
                    jnp.concatenate([query_low, zero], axis=1),
                    jnp.concatenate([zero, grad_low], axis=1),
                    jnp.concatenate([query_high, zero], axis=1),
                    jnp.concatenate([zero, grad_high], axis=1),
                ],
                axis=0,
            )
            adds = dot_nt(jnp.concatenate([grad_scores, chances.astype(BF)], axis=1), right)
            keys = jnp.concatenate([turned_of(low, kt_ref), turned_of(high, kt_ref)], axis=0)
            grad_query = dot_nn(keys, grad_scores)
            dq_ref[piece * tiles + tile] = jnp.where(left, grad_query[:DH], grad_query[DH:]) * (
                1.0 / math.sqrt(DH)
            )
            for side, blocks in enumerate((low, high)):
                for slot, b in enumerate(blocks):
                    at = pl.ds(pl.multiple_of(b * BLK, BLK), BLK)
                    acc_ref[at, :] += adds[slot * BLK : (slot + 1) * BLK, side * 128 : (side + 1) * 128]
        return carry

    lax.fori_loop(0, owners, step, 0)

    def finish(i, carry):
        at = pl.ds(pl.multiple_of(i * 128, 128), 128)
        d_ref[at, 0:128] = acc_ref[at, :].astype(BF)
        tile = jnp.concatenate([dq_ref[i], jnp.zeros((DH, 128), F32)], axis=0)
        d_ref[at, 128:256] = tile.T.astype(BF)
        return carry

    lax.fori_loop(0, rows // 128, finish, 0, unroll=4)


def attend_back(scalars, tables, grads):
    parts = len(tables[0])
    rows = sum(t.shape[0] for t in tables[0])
    anywhere = pl.BlockSpec(memory_space=pl.ANY)
    flat = [t for table in tables for t in table] + [grads]
    return pl.pallas_call(
        functools.partial(attend_back_kernel, parts),
        in_specs=[pl.BlockSpec(memory_space=pltpu.SMEM)] * 3 + [anywhere] * len(flat),
        out_specs=pl.BlockSpec(memory_space=pltpu.VMEM),
        out_shape=jax.ShapeDtypeStruct((rows, 256), BF),
        scratch_shapes=[
            pltpu.VMEM((rows + BLK, 128), BF),
            pltpu.VMEM((rows + BLK, 128), BF),
            pltpu.VMEM((rows // 128, 128, 128), BF),
            pltpu.VMEM((rows // BLK + 1, DH, 128), BF),
            pltpu.VMEM(grads.shape, BF),
            pltpu.VMEM((rows + BLK, 128), F32),
            pltpu.VMEM((rows // 128, DH, 128), F32),
            pltpu.SemaphoreType.DMA((len(flat),)),
        ],
        compiler_params=params(),
        name="attend_back",
    )(*scalars, *flat)


def out_kernel(att_ref, tok_ref, w_ref, vec_ref, mid_ref, n2_ref):
    width = tok_ref.shape[1]
    mid = (
        tok_ref[...].astype(F32)
        + dot_tn(att_ref[...].reshape(width, -1), w_ref[...].reshape(width, width))
        + vec_ref[0:1, :]
    )
    mid_ref[...] = mid
    normal, _ = normalize(mid)
    n2_ref[...] = (normal * vec_ref[1:2, :] + vec_ref[2:3, :]).astype(BF)


def whole(shape):
    return pl.BlockSpec(shape, lambda c: (0,) * len(shape))


def out_rows(weights):
    owners, rows, width = weights.shape
    own = width // owners
    return pl.BlockSpec((owners, own, width), lambda c: (0, rows // own - 1, 0))


def project_out(attended, tokens, weights, vectors):
    shape = tokens.shape
    return pl.pallas_call(
        out_kernel,
        grid=(1,),
        in_specs=[whole(attended.shape), whole(shape), out_rows(weights), whole(vectors.shape)],
        out_specs=[whole(shape)] * 2,
        out_shape=[jax.ShapeDtypeStruct(shape, F32), jax.ShapeDtypeStruct(shape, BF)],
        compiler_params=params("arbitrary"),
        name="project_out",
    )(attended, tokens, weights, vectors)


def feed_kernel(n2_ref, cot_ref, down_ref, up_ref, vec_ref, out_ref, gn_ref, hid_ref, pre_ref, gb_ref, acc_ref, acc_gn):
    chunk = pl.program_id(0)
    width = n2_ref.shape[1]
    w_up = up_ref[...].reshape(width, -1)
    w_down = down_ref[...].reshape(-1, width)
    pre = dot_nn(n2_ref[...], w_up) + vec_ref[pl.ds(4 + chunk, 1), :]
    root = math.sqrt(2.0 / math.pi)
    square = pre * pre
    bent = jnp.tanh(root * (pre + 0.044715 * (pre * square)))
    hidden = (0.5 * pre * (1.0 + bent)).astype(BF)
    slope = 0.5 * (1.0 + bent) + 0.5 * pre * (1.0 - bent * bent) * (
        root * (1.0 + (3 * 0.044715) * square)
    )
    grad_pre = (slope * dot_nt(cot_ref[...], w_down)).astype(BF)
    hid_ref[...] = hidden
    pre_ref[...] = grad_pre
    gb_ref[pl.ds(chunk, 1), :] = jnp.sum(grad_pre.astype(F32), axis=0, keepdims=True)
    more = dot_nn(hidden, w_down)
    grad_more = dot_nt(grad_pre, w_up)

    @pl.when(chunk == 0)
    def _():
        acc_ref[...] = more
        acc_gn[...] = grad_more

    @pl.when(chunk > 0)
    def _():
        out_ref[...] = (acc_ref[...] + more).astype(out_ref.dtype)
        gn_ref[...] = (acc_gn[...] + grad_more).astype(gn_ref.dtype)


def layout_of(weights):
    owners, rows, width = weights.shape
    own = width // owners
    units = (rows - own) // 2
    chunks = units // own
    return owners, own, width, units, chunks


def feed(normed, cotangent, weights, vectors, kind):
    owners, own, width, units, chunks = layout_of(weights)
    assert chunks == 2
    count = normed.shape[0]
    first_up = units // own
    column = pl.BlockSpec((count, width), lambda c: (0, c))
    wide = jax.ShapeDtypeStruct((count, chunks * width), BF)
    return pl.pallas_call(
        feed_kernel,
        grid=(chunks,),
        in_specs=[
            whole(normed.shape),
            whole(cotangent.shape),
            pl.BlockSpec((owners // chunks, units, width), lambda c: (c, 0, 0)),
            pl.BlockSpec((owners, own, width), lambda c: (0, first_up + c, 0)),
            whole(vectors.shape),
        ],
        out_specs=[whole((count, width))] * 2 + [column, column, whole((8, width))],
        out_shape=[
            jax.ShapeDtypeStruct((count, width), kind),
            jax.ShapeDtypeStruct((count, width), kind),
            wide,
            wide,
            jax.ShapeDtypeStruct((8, width), F32),
        ],
        scratch_shapes=[pltpu.VMEM((count, width), F32), pltpu.VMEM((count, width), F32)],
        compiler_params=params("arbitrary"),
        name="feed",
    )(normed, cotangent, weights, weights, vectors)


def feed_grads_kernel(na_ref, nb_ref, ca_ref, cb_ref, ha_ref, hb_ref, pa_ref, pb_ref, grads_hbm, gd_buf, gu_buf, sem):
    chunk = pl.program_id(0)
    down_block, down_rows = gd_buf.shape[1:3]
    up_rows = gu_buf.shape[2]
    down = dot_tn(ha_ref[...], ca_ref[...]) + dot_tn(hb_ref[...], cb_ref[...])
    gd_buf[chunk] = down.astype(BF).reshape(gd_buf.shape[1:])
    copy_down = lambda c: pltpu.make_async_copy(
        gd_buf.at[c],
        grads_hbm.at[pl.ds(c * down_block, down_block), pl.ds(0, down_rows)],
        sem.at[0, c],
    )
    copy_up = lambda c: pltpu.make_async_copy(
        gu_buf.at[c],
        grads_hbm.at[:, pl.ds(down_rows + c * up_rows, up_rows)],
        sem.at[1, c],
    )
    copy_down(chunk).start()
    up = dot_tn(na_ref[...], pa_ref[...]) + dot_tn(nb_ref[...], pb_ref[...])
    gu_buf[chunk] = up.astype(BF).reshape(gu_buf.shape[1:])
    copy_up(chunk).start()

    @pl.when(chunk == 1)
    def _():
        for c in range(2):
            copy_down(c).wait()
            copy_up(c).wait()


def feed_grads(own_part, other_part, weights):
    owners, own, width, units, chunks = layout_of(weights)
    count = own_part[0].shape[0]
    column = pl.BlockSpec((count, width), lambda c: (0, c))
    inputs = [t for both in zip(own_part, other_part) for t in both]
    return pl.pallas_call(
        feed_grads_kernel,
        grid=(chunks,),
        in_specs=[whole((count, width))] * 4 + [column] * 4,
        out_specs=pl.BlockSpec(memory_space=pl.ANY),
        out_shape=jax.ShapeDtypeStruct((owners, 2 * units, width), BF),
        scratch_shapes=[
            pltpu.VMEM((chunks, owners // chunks, units, width), BF),
            pltpu.VMEM((chunks, owners, own, width), BF),
            pltpu.SemaphoreType.DMA((2, chunks)),
        ],
        compiler_params=params("arbitrary"),
        name="feed_grads",
    )(*inputs)


def out_back_kernel(
    mid_ref, gn_ref, other_ref, cot_ref, att_ref, w_ref, vec_ref, gm_ref, ga_ref, gv_ref, gw_ref
):
    width = mid_ref.shape[1]
    normal, scale = normalize(mid_ref[...])
    grad = gn_ref[...] + other_ref[...].astype(F32)
    cot = cot_ref[...].astype(F32)
    grad_mid = cot + norm_backward(grad, normal, scale, vec_ref[1:2, :])
    gm_ref[...] = grad_mid
    branch = grad_mid.astype(BF)
    ga_ref[...] = dot_nt(w_ref[...].reshape(width, width), branch).astype(BF).reshape(ga_ref.shape)
    gw_ref[...] = dot_nn(att_ref[...].reshape(width, -1), branch).astype(BF).reshape(gw_ref.shape)
    gv_ref[...] = jnp.zeros_like(gv_ref)
    gv_ref[0:1, :] = jnp.sum(branch.astype(F32), axis=0, keepdims=True)
    gv_ref[1:2, :] = jnp.sum(grad * normal, axis=0, keepdims=True)
    gv_ref[2:3, :] = jnp.sum(grad, axis=0, keepdims=True)
    gv_ref[3:4, :] = jnp.sum(cot, axis=0, keepdims=True)


def project_out_back(mid, grad, other, cotangent, attended, weights, vectors):
    owners, own, width, units, chunks = layout_of(weights)
    shape = mid.shape
    packed = attended.shape
    return pl.pallas_call(
        out_back_kernel,
        grid=(1,),
        in_specs=[whole(shape)] * 4 + [whole(packed), out_rows(weights), whole(vectors.shape)],
        out_specs=[whole(shape), whole(packed), whole((8, width)), whole((owners, own, width))],
        out_shape=[
            jax.ShapeDtypeStruct(shape, F32),
            jax.ShapeDtypeStruct(packed, BF),
            jax.ShapeDtypeStruct((8, width), F32),
            jax.ShapeDtypeStruct((owners, own, width), BF),
        ],
        compiler_params=params("arbitrary"),
        name="project_out_back",
    )(mid, grad, other, cotangent, attended, weights, vectors)


def shares_kernel(starts, d_ref, w_ref, *outs):
    weight = w_ref[...]
    for start, out_ref in zip(starts, outs):
        out_ref[...] = dot_nt(d_ref[start : start + out_ref.shape[0], :], weight).astype(BF)


def head_shares(grad_table, weight, starts, count):
    width = weight.shape[0]
    return pl.pallas_call(
        functools.partial(shares_kernel, starts),
        out_shape=[jax.ShapeDtypeStruct((count, width), BF)] * len(starts),
        compiler_params=params(),
        name="head_shares",
    )(grad_table, weight)


def last_kernel(tok_ref, one_ref, two_ref, three_ref, four_ref, gm_ref, norm_ref, out_ref):
    step = 128

    def rows(i, carry):
        at = pl.ds(pl.multiple_of(i * step, step), step)
        normal, scale = normalize(tok_ref[at, :].astype(F32))
        terms = [ref[at, :].astype(F32) for ref in (one_ref, two_ref, three_ref, four_ref)]
        grad = (terms[0] + terms[1]) + (terms[2] + terms[3])
        out_ref[at, :] = (gm_ref[at, :] + norm_backward(grad, normal, scale, norm_ref[0:1, :])).astype(BF)
        return carry

    lax.fori_loop(0, tok_ref.shape[0] // step, rows, 0)


def last(tokens, terms, grad_middle, norm_rows):
    return pl.pallas_call(
        last_kernel,
        out_shape=jax.ShapeDtypeStruct(tokens.shape, BF),
        compiler_params=params(),
        name="last",
    )(tokens, *terms, grad_middle, norm_rows)


def exchange(table):
    return lax.all_to_all(table, "shard", split_axis=0, concat_axis=0, tiled=True)


def trade(table):
    reps = lax.axis_size("rep")
    return lax.ppermute(table, "rep", [(r, r ^ 1) for r in range(reps)])


def over_alike(table):
    reps = lax.axis_size("rep")
    if reps == 2:
        return table
    groups = [list(range(first, reps, 2)) for first in range(2)]
    return lax.psum(table, "rep", axis_index_groups=groups)


def local(
    ring,
    tokens,
    cotangent,
    seg_ids,
    random_blocks,
    global_blocks,
    ln1_gain,
    ln1_bias,
    w_query,
    b_query,
    w_key,
    w_value,
    b_value,
    w_out,
    b_out,
    ln2_gain,
    ln2_bias,
    w_up,
    b_up,
    w_down,
    b_down,
):
    tokens, cotangent, seg_row = tokens[0], cotangent[0], seg_ids[0]
    count, width = tokens.shape
    owners = lax.axis_size("shard")
    own = width // owners
    hidden = w_up.shape[1]
    units = hidden // owners // 2
    half = lax.axis_index("rep") % 2

    tiles = jnp.concatenate(
        [w.reshape(own, owners, DH) for w in (w_key, w_value, w_query)], axis=2
    ).transpose(1, 0, 2)
    small = jnp.concatenate([b_out, ln2_gain, ln2_bias, b_down, ln1_gain, ln1_bias, b_up])
    small = jnp.pad(small, (0, own * DH - small.shape[0])).reshape(1, own, DH)
    sent = jnp.concatenate([tiles, jnp.broadcast_to(small, (owners, own, DH))], axis=2)
    got = exchange(sent)
    weight = jnp.pad(got[:, :, : 3 * DH], ((0, 0), (0, 0), (0, DH))).reshape(width, 4 * DH)
    rows = got[:, :, 3 * DH :].reshape(owners, own * DH)[:, : 6 * own + hidden // owners]
    rows = rows.astype(F32)
    fixed = rows[:, : 6 * own].reshape(owners, 6, own).transpose(1, 0, 2).reshape(6, width)
    up_bias = lax.dynamic_slice_in_dim(rows[:, 6 * own :], half * units, units, axis=1)
    vectors = jnp.concatenate([fixed[:4], up_bias.reshape(2, width), jnp.zeros((2, width), F32)], axis=0)
    norm_rows = jnp.pad(fixed[4:6], ((0, 6), (0, 0)))
    zero = jnp.zeros((DH,), F32)
    bias = jnp.concatenate([zero, b_value.astype(F32), b_query.astype(F32), zero])
    bias = jnp.broadcast_to(bias[None], (8, 4 * DH))

    up_half = lax.dynamic_index_in_dim(w_up.reshape(own, owners, 2, units), half, 2, keepdims=False)
    mine = jnp.concatenate(
        [
            lax.dynamic_slice_in_dim(w_down, half * units, units, axis=0),
            up_half.reshape(own, 2, width).transpose(1, 0, 2).reshape(2 * own, width),
            w_out,
        ],
        axis=0,
    )
    other_cotangent = trade(cotangent)

    per = count // BLK
    sources = ring.sources()
    idx = key_blocks(random_blocks[0, 0], global_blocks[0])
    position = jnp.arange(owners, dtype=jnp.int32)
    piece_of = jnp.sum(jnp.where(sources[None] == position[:, None], position[None], 0), axis=1)
    place = piece_of[:, None] * per + jnp.arange(per, dtype=jnp.int32)[None]
    place = jnp.concatenate([place.reshape(-1), jnp.full((1,), owners * per, jnp.int32)])
    scalars = (idx.reshape(-1), sources, place)
    segs = seg_row.reshape(owners, count)[sources]

    def use(stage, pieces, ready):
        first = sum(len(earlier) for earlier in ring.stages[:stage])
        segs_here = jnp.pad(segs[first : first + len(pieces)], ((0, 8 - len(pieces)), (0, 0)))
        return project(pieces, segs_here, *ready)

    gathered = []

    def gate(rows):
        own_weights, rows = lax.optimization_barrier((mine, rows))
        gathered.append(lax.all_gather(own_weights, "shard", axis=0))
        return rows

    projected = ring.gather(tokens, use, (weight, bias, norm_rows), gate, min(GATE, ring.far))
    weights = gathered[0]
    projected, other_cotangent = lax.optimization_barrier((projected, other_cotangent))
    table = lambda *which: [[stage[i] for stage in projected] for i in which]
    attended = exchange(attend(scalars, table(1, 3, 5), owners))
    mid, normed_two = project_out(attended, tokens, weights, vectors)
    other_normed = trade(normed_two)
    more, grad_two, hid, grad_pre, bias_one = feed(normed_two, cotangent, weights, vectors, F32)
    other_normed, grad_two = lax.optimization_barrier((other_normed, grad_two))
    other_more, other_grad, other_hid, other_pre, bias_two = feed(
        other_normed, other_cotangent, weights, vectors, BF
    )
    other_grad = trade(other_grad)
    other_more = trade(other_more)
    grads = feed_grads(
        (normed_two, cotangent, hid, grad_pre),
        (other_normed, other_cotangent, other_hid, other_pre),
        weights,
    )
    other_grad, grads = lax.optimization_barrier((other_grad, grads))
    grad_middle, grad_attended, grad_rows, grad_out = project_out_back(
        mid, grad_two, other_grad, cotangent, attended, weights, vectors
    )
    layer_out = (mid + more + other_more.astype(F32) + fixed[3][None]).astype(BF)
    summed = lambda t: lax.psum_scatter(t.reshape(-1, width), "shard", scatter_dimension=0, tiled=True)
    shares = summed(grads)
    shares, grad_out = lax.optimization_barrier((shares, grad_out))
    out_share = summed(grad_out)
    grad_table = attend_back(scalars, table(1, 2, 3, 4), exchange(grad_attended))
    at = {piece: i * count for i, piece in enumerate(ring.pieces)}
    order = ring.scatter_order()
    other_shares = head_shares(grad_table, weight, [at[k, 1] for k in order], count)
    table_later, _ = lax.optimization_barrier((grad_table, other_shares))
    own_shares = head_shares(table_later, weight, [at[k, 0] for k in order], count)
    results = []

    def release(first):
        first, table = lax.optimization_barrier((first, grad_table))
        results.append(weight_grads(table))
        return first

    def weight_grads(table):
        grad_weight, done = 0.0, 0
        for stage in projected:
            normed = stage[0]
            grad_weight = grad_weight + dot_tn(normed, table[done : done + normed.shape[0]])
            done += normed.shape[0]
        return finish_weights(grad_weight, jnp.sum(table.astype(F32), axis=0, keepdims=True))

    def finish(rows):
        tied = lax.optimization_barrier((rows, results[0]))
        results[0] = tied[1]
        return tied[0]

    def finish_weights(grad_weight, grad_bias):
        used = weight.astype(F32)[:, : 3 * DH]
        sums = grad_bias[0:1, : 3 * DH]
        spread = grad_weight[:, : 3 * DH] - fixed[5][:, None] * sums
        grad_gain = jnp.sum(used * spread, axis=1) / fixed[4]
        grad_shift = jnp.sum(used * sums, axis=1)
        lines = jnp.concatenate([grad_rows[:4], grad_gain[None], grad_shift[None]], axis=0)
        lines = lines.reshape(6, owners, own).transpose(1, 0, 2).reshape(owners, 6 * own)
        up_lines = (bias_one[:2] + bias_two[:2]).reshape(owners, units)
        lines = jnp.concatenate([lines, up_lines], axis=1)
        length = lines.shape[1]
        lines = jnp.pad(lines, ((0, 0), (0, own * DH - length))).reshape(owners, own, DH)
        back = jnp.concatenate(
            [grad_weight[:, : 3 * DH].reshape(owners, own, 3 * DH), lines], axis=2
        ).astype(BF)
        back = exchange(back)
        back_sum = jnp.sum(back[:, :, 3 * DH :].astype(F32), axis=0).reshape(own * DH)[:length]
        heads = over_alike(back[:, :, : 3 * DH])
        heads = heads.astype(F32) + trade(heads).astype(F32)
        heads = heads.transpose(1, 2, 0).reshape(own, 3, DH, owners).transpose(1, 0, 3, 2)
        heads = heads.reshape(3, own, width)
        tail = jnp.concatenate([back_sum, grad_bias[0, 2 * DH : 3 * DH], grad_bias[0, DH : 2 * DH]])
        tail = over_alike(tail.astype(BF))
        tail_other = trade(tail).astype(F32)
        tail = tail.astype(F32)
        total = tail + tail_other
        piece = lambda i: total[i * own : (i + 1) * own]

        def in_order(here, there, axis):
            both = [jnp.where(half == 0, here, there), jnp.where(half == 0, there, here)]
            return jnp.stack(both, axis=axis)

        grad_up_bias = in_order(tail[6 * own : length], tail_other[6 * own : length], 0).reshape(-1)
        ours = over_alike(shares)
        theirs = trade(ours)
        ours, theirs = ours.astype(F32), theirs.astype(F32)
        grad_down = in_order(ours[:units], theirs[:units], 0).reshape(2 * units, width)
        up_of = lambda t: t[units : 2 * units].reshape(2, own, width).transpose(1, 0, 2).reshape(
            own, owners, units
        )
        grad_up = in_order(up_of(ours), up_of(theirs), 2).reshape(own, hidden)
        out_sum = over_alike(out_share)
        grad_out = out_sum.astype(F32) + trade(out_sum).astype(F32)
        return (
            piece(4),
            piece(5),
            heads[2],
            total[length : length + DH],
            heads[0],
            heads[1],
            total[length + DH :],
            grad_out,
            piece(0),
            piece(1),
            piece(2),
            grad_up,
            grad_up_bias,
            grad_down,
            piece(3),
        )

    terms = ring.scatter_sum(
        dict(zip(order, own_shares)), dict(zip(order, other_shares)), release, finish
    )
    grad_tokens = last(tokens, terms, grad_middle, norm_rows)
    return (layer_out[None], grad_tokens[None], *results[0])


def solution(mesh):
    rows = P("rep", "shard", None)
    one, two = P("shard"), P("shard", None)
    return jax.shard_map(
        functools.partial(local, Ring(ring_of(mesh))),
        mesh=mesh,
        in_specs=(
            rows, rows, P("rep", None), P("rep", "shard", None, None), P("rep", None),
            one, one, two, one, two, two, one, two, one, one, one, two, one, two, one,
        ),
        out_specs=(
            rows, rows, one, one, two, one, two, two, one, two, one, one, one, two, one, two, one,
        ),
        check_vma=False,
    )
```
